128 devices in a mesh: ang: 16 (over z_lo, x, core), img: 8 (over z_hi, y).
Axes of the slice: x: 4, y: 4, z: 4 (z_hi: 2, z_lo: 2; z = z_hi * 2 + z_lo), core: 2. Of those that a mesh axis runs over, the one named last changes fastest.
Arguments:
- sinogram: bfloat16 [32, 64, 4096], P('ang', None, 'img'), may hold values from -4 to 28
- offsets: int32 [32], replicated, may hold values from 0 to 65504, as said below
- steps: int32 [32, 2], replicated, may hold values from -32 to 32, as said below
Outputs:
- picture: bfloat16 [1024, 64, 1024], P('ang', None, 'img')
The draws below stay inside these ranges and needn't reach their ends.
Inputs may be any that keep to these rules, and one draw needn't show every extreme that they name: Each row (u, v) of steps satisfies u^2 + v^2 <= 32^2 < (|u| + 1)^2 + (|v| + 1)^2. For every angle a and every pixel (y, x) with 0 <= x, y < 1024, offsets[a] + steps[a, 0] x + steps[a, 1] y lies in 0 to 65504.
All inputs are finite; a program needn't handle non-finite values.
Results may differ from the reference program's by a relative error of at most 0.0053.
Values may be sent and summed in bfloat16 or wider, within the bound.
A program may use at most 192 MiB of HBM per device.

```python
import math
import jax
import jax.numpy as jnp
from jax import lax

BINS = 4096
IMG = 1024
SLICES = 64
ANGLES = 32
STEP_MAX = 32


def lattice_steps(key):
    base_key = jax.random.fold_in(key, 5417)
    key_first, key_sign, key_swap = jax.random.split(base_key, 3)
    first_part = jax.random.randint(key_first, (ANGLES,), -STEP_MAX, STEP_MAX + 1, dtype=jnp.int32)
    remains = STEP_MAX * STEP_MAX - first_part * first_part
    counter = jnp.arange(1, STEP_MAX + 1, dtype=jnp.int32)
    magnitude = jnp.sum((counter[None, :] * counter[None, :] <= remains[:, None]).astype(jnp.int32), axis=1).astype(jnp.int32)
    sign_value = jax.random.randint(key_sign, (ANGLES,), 0, 2, dtype=jnp.int32) * 2 - 1
    second_part = sign_value * magnitude
    swapped = jax.random.randint(key_swap, (ANGLES,), 0, 2, dtype=jnp.int32) == 1
    along_x = jnp.where(swapped, second_part, first_part)
    along_y = jnp.where(swapped, first_part, second_part)
    angle_order = jnp.arange(ANGLES, dtype=jnp.int32)
    along_x = jnp.where(angle_order == 0, -jnp.abs(along_x), jnp.where(angle_order == 1, jnp.abs(along_x), along_x))
    along_y = jnp.where(angle_order == 0, -jnp.abs(along_y), jnp.where(angle_order == 1, jnp.abs(along_y), along_y))
    return jnp.stack([along_x, along_y], axis=1).astype(jnp.int32)


def geometry(key):
    step_pairs = lattice_steps(key)
    key_room = jax.random.fold_in(key, 7321)
    spread = (IMG - 1) * (jnp.abs(step_pairs[:, 0]) + jnp.abs(step_pairs[:, 1]))
    spare_room = 16 * (BINS - 2) - spread
    shift_in = jax.random.randint(key_room, (ANGLES,), 0, spare_room + 1, dtype=jnp.int32)
    angle_order = jnp.arange(ANGLES, dtype=jnp.int32)
    shift_in = jnp.where(angle_order == 0, spare_room, jnp.where(angle_order == 1, 0, shift_in))
    anchor = shift_in - (IMG - 1) * (jnp.minimum(step_pairs[:, 0], 0) + jnp.minimum(step_pairs[:, 1], 0))
    return (anchor.astype(jnp.int32), step_pairs)


def draw_offsets(key, part):
    return geometry(key)[0]


def draw_steps(key, part):
    return geometry(key)[1]


def bump_profile(bins_axis, center, half_width, height):
    ratio = (bins_axis - center) / half_width
    return height * jnp.sqrt(jnp.maximum(1.0 - ratio * ratio, 0.0))


def draw_sinogram(key, part):
    base_key = jax.random.fold_in(key, 911)
    key_list = jax.random.split(base_key, 16)
    row_shape = (ANGLES, SLICES, 1)
    bins_axis = jnp.arange(BINS, dtype=jnp.float32)[None, None, :]
    rough_part = jnp.clip(jax.random.normal(key_list[1], (ANGLES, SLICES, BINS), jnp.float32), -4.0, 4.0)
    body_low, body_high = (3.0, 6.0)
    small_low, small_high = (1.5, 4.0)
    summed = rough_part
    body_half = BINS * jax.random.uniform(key_list[2], row_shape, jnp.float32, 0.25, 0.45)
    body_center = body_half + jax.random.uniform(key_list[3], row_shape, jnp.float32) * (BINS - 2.0 * body_half)
    body_height = jax.random.uniform(key_list[4], row_shape, jnp.float32, body_low, body_high)
    summed = summed + bump_profile(bins_axis, body_center, body_half, body_height)
    for which in range(3):
        half_width = BINS * jnp.exp(jax.random.uniform(key_list[5 + 3 * which], row_shape, jnp.float32, math.log(1.0 / 16.0), math.log(0.25)))
        center = half_width + jax.random.uniform(key_list[6 + 3 * which], row_shape, jnp.float32) * (BINS - 2.0 * half_width)
        height = jax.random.uniform(key_list[7 + 3 * which], row_shape, jnp.float32, small_low, small_high)
        summed = summed + bump_profile(bins_axis, center, half_width, height)
    return summed.astype(jnp.bfloat16)


def setup_inputs(seed: int = 0) -> dict:
    streams_of = jax.random.split(jax.random.key(seed), 4)
    sinogram = draw_sinogram(jax.random.fold_in(streams_of[3], 71), 0)
    offsets = draw_offsets(jax.random.fold_in(streams_of[3], 71), 0)
    steps = draw_steps(jax.random.fold_in(streams_of[3], 71), 0)
    return dict(sinogram=sinogram, offsets=offsets, steps=steps)


def ramp_table():
    bin_index = jnp.arange(BINS, dtype=jnp.int32)
    offset_gap = bin_index[None, :] - bin_index[:, None]
    safe_gap = jnp.where(offset_gap == 0, 1, offset_gap).astype(jnp.float32)
    odd_gap = offset_gap % 2 != 0
    kernel = jnp.where(offset_gap == 0, jnp.float32(0.25), jnp.where(odd_gap, -1.0 / (math.pi ** 2 * safe_gap * safe_gap), jnp.float32(0.0)))
    return kernel.astype(jnp.float32)

def reference(sinogram, offsets, steps):
    ramp_rows = ramp_table()
    filtered = jnp.dot(sinogram.reshape(-1, BINS).astype(jnp.float32), ramp_rows, precision=lax.Precision.HIGHEST, preferred_element_type=jnp.float32)
    filtered = filtered.astype(jnp.bfloat16).reshape(sinogram.shape)
    rows_iota = jnp.arange(IMG, dtype=jnp.int32)
    cols_iota = jnp.arange(IMG, dtype=jnp.int32)

    def one_angle(summed, angle_data):
        filtered_one, offset, step_pair = angle_data
        position = offset + step_pair[0] * cols_iota[None, :] + step_pair[1] * rows_iota[:, None]
        low_bin = (position // 16).astype(jnp.int32)
        upper_weight = (position % 16).astype(jnp.float32) / 16.0
        values = filtered_one.astype(jnp.float32)
        lower_val = jnp.take(values, low_bin.reshape(-1), axis=1).reshape(SLICES, IMG, IMG)
        upper_val = jnp.take(values, (low_bin + 1).reshape(-1), axis=1).reshape(SLICES, IMG, IMG)
        contrib = (1.0 - upper_weight)[None] * lower_val + upper_weight[None] * upper_val
        return (summed + jnp.transpose(contrib, (1, 0, 2)), None)
    start_sum = jnp.zeros((IMG, SLICES, IMG), jnp.float32)
    summed = lax.scan(one_angle, start_sum, (filtered, offsets, steps))[0]
    return (summed * (2.0 / math.sqrt(ANGLES))).astype(jnp.bfloat16)
```

```python
import math

import jax
import jax.numpy as jnp
from jax import lax
from jax.experimental import pallas as pl
from jax.experimental.pallas import tpu as pltpu
from jax.sharding import PartitionSpec as P

BINS = 4096
IMG = 1024
ANGLES = 32
SLICES = 64
ANG = 16
IMGD = 8
CHIPS = 64
ROWS = IMG // ANG
COLS = IMG // IMGD
TILE = 32
GROUP = 16
MESH = pl.DeviceIdType.MESH
VMEM = pl.BlockSpec(memory_space=pltpu.VMEM)
SMEM = pl.BlockSpec(memory_space=pltpu.SMEM)
LIMIT = 48 * 1024 * 1024


def exchange_rows(sino, recv, local_sem, send_sem, recv_sem):
    i = lax.axis_index("ang")
    j = lax.axis_index("img")
    barrier = pltpu.get_barrier_semaphore()
    for k in range(1, IMGD):
        pl.semaphore_signal(barrier, inc=1, device_id=(i, lax.rem(j + k, IMGD)), device_id_type=MESH)
    own = pltpu.make_async_copy(sino.at[j], recv.at[j], local_sem)
    own.start()
    pl.semaphore_wait(barrier, IMGD - 1)

    def copy(k):
        to = lax.rem(j + k, IMGD)
        return pltpu.make_async_remote_copy(
            src_ref=sino.at[to],
            dst_ref=recv.at[j],
            send_sem=send_sem.at[k],
            recv_sem=recv_sem.at[k],
            device_id=(i, to),
            device_id_type=MESH,
        )

    copies = [copy(k) for k in range(1, IMGD)]
    for c in copies:
        c.start()
    own.wait()
    for c in copies:
        c.wait()


def ramp_tiles(ramp_hi, ramp_fine):
    gap = lax.broadcasted_iota(jnp.int32, (128, 128), 1) - lax.broadcasted_iota(jnp.int32, (128, 128), 0)
    scale = jnp.where((gap & 1) != 0, jnp.float32(-1.0 / math.pi**2), jnp.float32(0.0))
    gap_f = gap.astype(jnp.float32)

    def value(e):
        t = gap_f + jnp.asarray(128 * e).astype(jnp.float32)
        t = jnp.where(t == 0.0, jnp.float32(1.0), t)
        return scale / (t * t)

    @pl.loop(0, 64)
    def _(e):
        ramp_hi[e] = value(e - 32).astype(jnp.bfloat16)

    for e in range(-3, 4):
        v = value(e)
        if e == 0:
            v = jnp.where(gap == 0, jnp.float32(0.25), v)
        hi = v.astype(jnp.bfloat16)
        rest = v - hi.astype(jnp.float32)
        mid = rest.astype(jnp.bfloat16)
        low = (rest - mid.astype(jnp.float32)).astype(jnp.bfloat16)
        ramp_hi[e + 32] = hi
        ramp_fine[0, e + 3] = mid
        ramp_fine[1, e + 3] = low


def toeplitz(tiles, at):
    top = jnp.concatenate([tiles[at], tiles[at + 1]], axis=1)
    low = jnp.concatenate([tiles[at - 1], tiles[at]], axis=1)
    return jnp.concatenate([top, low], axis=0)


def filter_rows(x, acc, ramp_hi, ramp_fine):
    acc[...] = jnp.zeros_like(acc)
    for d in sorted(range(-15, 16), key=abs):
        count = 16 - abs(d)
        lhs = x[pl.ds(max(0, -d), count)].reshape(count * GROUP, 256)
        total = jnp.dot(lhs, toeplitz(ramp_hi, 2 * d + 32), preferred_element_type=jnp.float32)
        if abs(d) <= 1:
            for term in range(2):
                total += jnp.dot(
                    lhs, toeplitz(ramp_fine.at[term], 2 * d + 3), preferred_element_type=jnp.float32
                )
        acc[pl.ds(max(0, d), count)] += total.reshape(count, GROUP, 256)


def angle_data(offsets, steps, a):
    u = steps[a, 0]
    v = steps[a, 1]
    return offsets[a], u, v, jnp.minimum(u, 0) + jnp.minimum(v, 0)


def window_start(offset, u, v, low, chip_row, img):
    return (offset + u * (COLS * img) + v * (2 * ROWS * chip_row) + low * 127) >> 4


def pack_windows(filt, packed, offsets, steps):
    i = lax.axis_index("ang")
    j = lax.axis_index("img")
    offset, u, v, low = angle_data(offsets, steps, 2 * i + j // 4)
    lane = lax.broadcasted_iota(jnp.int32, (GROUP, 128), 1)

    @pl.loop(0, CHIPS)
    def _(d):
        ws = window_start(offset, u, v, low, d // IMGD, d % IMGD)
        shift = ws & 127
        blocks = filt[pl.ds(ws >> 7, 4)]
        back = (128 - shift) & 127
        rolled = [pltpu.roll(blocks[k], back, 1) for k in range(4)]
        for k in range(3):
            packed[d, k] = jnp.where(lane < 128 - shift, rolled[k], rolled[k + 1]).astype(jnp.bfloat16)


def filter_kernel(offsets, steps, recv, packed, ramp_hi, ramp_fine, x, acc, filt):
    ramp_tiles(ramp_hi, ramp_fine)
    for b in range(16):
        x[b] = recv[b // 2, :, pl.ds(256 * (b % 2), 256)]
    filter_rows(x, acc, ramp_hi, ramp_fine)
    for b in range(16):
        for h in range(2):
            filt[2 * b + h] = acc[b, :, pl.ds(128 * h, 128)]
    filt[pl.ds(32, 4)] = jnp.zeros((4, GROUP, 128), jnp.float32)
    pack_windows(filt, packed, offsets, steps)


def exchange_windows(packed, recv, local_sem, send_sem, recv_sem, sib_send, sib_recv):
    i = lax.axis_index("ang")
    j = lax.axis_index("img")
    core = lax.rem(i, 2)
    row = i // 2
    me = row * IMGD + j
    barrier = pltpu.get_barrier_semaphore()

    @pl.loop(1, CHIPS)
    def _(k):
        to = lax.rem(me + k, CHIPS)
        pl.semaphore_signal(
            barrier, inc=1, device_id=(2 * (to // IMGD) + core, lax.rem(to, IMGD)), device_id_type=MESH
        )

    sibling = (2 * row + 1 - core, j)
    pl.semaphore_signal(barrier, inc=1, device_id=sibling, device_id_type=MESH)
    own = pltpu.make_async_copy(packed.at[me], recv.at[core, row, j], local_sem)
    own.start()
    pl.semaphore_wait(barrier, CHIPS)

    def copy(k):
        to = lax.rem(me + k, CHIPS)
        return pltpu.make_async_remote_copy(
            src_ref=packed.at[to],
            dst_ref=recv.at[core, row, j],
            send_sem=send_sem.at[k],
            recv_sem=recv_sem.at[k],
            device_id=(2 * (to // IMGD) + core, lax.rem(to, IMGD)),
            device_id_type=MESH,
        )

    @pl.loop(1, CHIPS)
    def _(k):
        copy(k).start()

    own.wait()

    @pl.loop(1, CHIPS)
    def _(k):
        copy(k).wait()

    share = pltpu.make_async_remote_copy(
        src_ref=recv.at[core],
        dst_ref=recv.at[core],
        send_sem=sib_send,
        recv_sem=sib_recv,
        device_id=sibling,
        device_id_type=MESH,
    )
    share.start()
    share.wait()


def project_kernel(offsets, steps, recv, out, lhs, weights, acc):
    i = lax.axis_index("ang")
    j = lax.axis_index("img")
    lane = lax.broadcasted_iota(jnp.int32, (1, 128), 1)
    pixel = lax.broadcasted_iota(jnp.int32, (1, TILE * TILE), 1)
    px = (pixel & (TILE - 1)).astype(jnp.float32)
    py = (pixel >> 5).astype(jnp.float32)
    slot = lax.broadcasted_iota(jnp.int32, (128, TILE * TILE), 0).astype(jnp.float32)
    acc[...] = jnp.zeros_like(acc)

    @pl.loop(0, ANGLES // 2)
    def _(pair):
        source = (pair % 8) * 4 + (pair // 8) * 2
        for a in range(2):
            offset, u, v, low = angle_data(offsets, steps, source + a)
            first = ((offset + low * (TILE - 1)) & 15) - low * (TILE - 1)
            where = (first.astype(jnp.float32) + u.astype(jnp.float32) * px + v.astype(jnp.float32) * py) * 0.0625
            weights[pl.ds(128 * a, 128)] = jnp.maximum(1.0 - jnp.abs(slot - where), 0.0).astype(jnp.bfloat16)
            ws = window_start(offset, u, v, low, i // 2, j)
            for tile in range(8):
                ty, tx = tile // 4, tile % 4
                corner = offset + u * (COLS * j + TILE * tx) + v * (ROWS * i + TILE * ty) + low * (TILE - 1)
                begin = (corner >> 4) - ws
                block = begin >> 7
                shift = begin & 127
                back = (128 - shift) & 127
                after = jnp.minimum(block + 1, 2)
                for g in range(4):
                    left = recv[2 * pair + a, g, block].astype(jnp.float32)
                    right = recv[2 * pair + a, g, after].astype(jnp.float32)
                    left = pltpu.roll(left, back, 1)
                    right = pltpu.roll(right, back, 1)
                    band = jnp.where(lane < 128 - shift, left, right).astype(jnp.bfloat16)
                    lhs[pl.ds(tile * SLICES + g * GROUP, GROUP), pl.ds(128 * a, 128)] = band
        acc[...] += jnp.dot(lhs[...], weights[...], preferred_element_type=jnp.float32)

    scale = jnp.float32(2.0 / math.sqrt(ANGLES))
    near = lane < 64
    even = (lane & 32) == 0

    @pl.loop(0, 8)
    def _(g):
        for ty in range(2):
            for sg in range(4):
                v = [
                    acc[
                        pl.ds((ty * 4 + tx) * SLICES + sg * GROUP, GROUP),
                        pl.ds(pl.multiple_of(g * 128, 128), 128),
                    ]
                    * scale
                    for tx in range(4)
                ]
                for t in range(2):
                    p, q = v[t], v[t + 2]
                    v[t] = jnp.where(near, p, pltpu.roll(q, 64, 1))
                    v[t + 2] = jnp.where(near, pltpu.roll(p, 64, 1), q)
                for t in (0, 2):
                    p, q = v[t], v[t + 1]
                    v[t] = jnp.where(even, p, pltpu.roll(q, 32, 1))
                    v[t + 1] = jnp.where(even, pltpu.roll(p, 96, 1), q)
                for q in range(4):
                    out[TILE * ty + 4 * g + q, pl.ds(sg * GROUP, GROUP)] = v[q].astype(jnp.bfloat16)


def shards(sinogram, offsets, steps):
    rows = pl.pallas_call(
        exchange_rows,
        out_shape=jax.ShapeDtypeStruct((IMGD, GROUP, BINS // IMGD), jnp.bfloat16),
        in_specs=[VMEM],
        out_specs=VMEM,
        scratch_shapes=[
            pltpu.SemaphoreType.DMA,
            pltpu.SemaphoreType.DMA((IMGD,)),
            pltpu.SemaphoreType.DMA((IMGD,)),
        ],
        compiler_params=pltpu.CompilerParams(collective_id=0, has_side_effects=True),
        name="exchange_rows",
    )(sinogram.reshape(IMGD, GROUP, BINS // IMGD))
    packed = pl.pallas_call(
        filter_kernel,
        out_shape=jax.ShapeDtypeStruct((CHIPS, 3, GROUP, 128), jnp.bfloat16),
        in_specs=[SMEM, SMEM, VMEM],
        out_specs=VMEM,
        scratch_shapes=[
            pltpu.VMEM((64, 128, 128), jnp.bfloat16),
            pltpu.VMEM((2, 7, 128, 128), jnp.bfloat16),
            pltpu.VMEM((16, GROUP, 256), jnp.bfloat16),
            pltpu.VMEM((16, GROUP, 256), jnp.float32),
            pltpu.VMEM((36, GROUP, 128), jnp.float32),
        ],
        compiler_params=pltpu.CompilerParams(vmem_limit_bytes=LIMIT),
        name="filter_pack",
    )(offsets, steps, rows)
    windows = pl.pallas_call(
        exchange_windows,
        out_shape=jax.ShapeDtypeStruct((2, 8, IMGD, 3, GROUP, 128), jnp.bfloat16),
        in_specs=[VMEM],
        out_specs=VMEM,
        scratch_shapes=[
            pltpu.SemaphoreType.DMA,
            pltpu.SemaphoreType.DMA((CHIPS,)),
            pltpu.SemaphoreType.DMA((CHIPS,)),
            pltpu.SemaphoreType.DMA,
            pltpu.SemaphoreType.DMA,
        ],
        compiler_params=pltpu.CompilerParams(collective_id=1, has_side_effects=True, vmem_limit_bytes=LIMIT),
        name="exchange_windows",
    )(packed)
    return pl.pallas_call(
        project_kernel,
        out_shape=jax.ShapeDtypeStruct((ROWS, SLICES, COLS), jnp.bfloat16),
        in_specs=[SMEM, SMEM, VMEM],
        out_specs=VMEM,
        scratch_shapes=[
            pltpu.VMEM((8 * SLICES, 256), jnp.bfloat16),
            pltpu.VMEM((256, TILE * TILE), jnp.bfloat16),
            pltpu.VMEM((8 * SLICES, TILE * TILE), jnp.float32),
        ],
        compiler_params=pltpu.CompilerParams(vmem_limit_bytes=LIMIT),
        name="project",
    )(offsets, steps, windows.reshape(ANGLES, 4, 3, GROUP, 128))


def solution(mesh):
    return jax.shard_map(
        shards,
        mesh=mesh,
        in_specs=(P("ang", None, "img"), P(), P()),
        out_specs=P("ang", None, "img"),
        check_vma=False,
    )
```

```python
import math

import jax
import jax.numpy as jnp
from jax import lax
from jax.experimental import pallas as pl
from jax.experimental.pallas import tpu as pltpu
from jax.sharding import PartitionSpec as P

BINS = 4096
IMG = 1024
ANGLES = 32
SLICES = 64
ANG = 16
IMGD = 8
CHIPS = 64
ROWS = IMG // ANG
COLS = IMG // IMGD
TILE = 32
TILES = 8
GROUP = 16
PACK = 4
MESH = pl.DeviceIdType.MESH
LIMIT = 48 * 1024 * 1024


def ramp_tiles(ramp_hi, ramp_fine):
    gap = lax.broadcasted_iota(jnp.int32, (128, 128), 1) - lax.broadcasted_iota(jnp.int32, (128, 128), 0)
    scale = jnp.where((gap & 1) != 0, jnp.float32(-1.0 / math.pi**2), jnp.float32(0.0))
    gap_f = gap.astype(jnp.float32)

    def value(e):
        t = gap_f + jnp.asarray(128 * e).astype(jnp.float32)
        t = jnp.where(t == 0.0, jnp.float32(1.0), t)
        return scale / (t * t)

    @pl.loop(0, 64)
    def _(e):
        ramp_hi[e] = value(e - 32).astype(jnp.bfloat16)

    for e in range(-3, 4):
        v = value(e)
        if e == 0:
            v = jnp.where(gap == 0, jnp.float32(0.25), v)
        hi = v.astype(jnp.bfloat16)
        rest = v - hi.astype(jnp.float32)
        mid = rest.astype(jnp.bfloat16)
        low = (rest - mid.astype(jnp.float32)).astype(jnp.bfloat16)
        ramp_hi[e + 32] = hi
        ramp_fine[0, e + 3] = mid
        ramp_fine[1, e + 3] = low


def toeplitz(tiles, at):
    top = jnp.concatenate([tiles[at], tiles[at + 1]], axis=1)
    low = jnp.concatenate([tiles[at - 1], tiles[at]], axis=1)
    return jnp.concatenate([top, low], axis=0)


def filter_rows(rows, acc, filt, ramp_hi, ramp_fine):
    for d in sorted(range(-15, 16), key=abs):
        count = 16 - abs(d)
        first = max(0, -d)
        lhs = jnp.concatenate(
            [rows[b // 2, :, pl.ds(256 * (b % 2), 256)] for b in range(first, first + count)], axis=0
        )
        total = jnp.dot(lhs, toeplitz(ramp_hi, 2 * d + 32), preferred_element_type=jnp.float32)
        if abs(d) <= 1:
            for term in range(2):
                total += jnp.dot(
                    lhs, toeplitz(ramp_fine.at[term], 2 * d + 3), preferred_element_type=jnp.float32
                )
        total = total.reshape(count, GROUP, 256)
        if d == 0:
            acc[...] = total
        else:
            acc[pl.ds(max(0, d), count)] += total
    for b in range(16):
        for h in range(2):
            filt[2 * b + h] = acc[b, :, pl.ds(128 * h, 128)].astype(jnp.bfloat16)
    filt[pl.ds(32, 4)] = jnp.zeros((4, GROUP, 128), jnp.bfloat16)


def angle_data(offsets, steps, a):
    u = steps[0, a]
    v = steps[1, a]
    return offsets[a], u, v, jnp.minimum(u, 0) + jnp.minimum(v, 0)


def window_start(offset, u, v, low, chip_row, img):
    return (offset + u * (COLS * img) + v * (2 * ROWS * chip_row) + low * 127) >> 4


def place_lhs(part, lhs, offsets, steps, angle_of):
    i = lax.axis_index("ang")
    j = lax.axis_index("img")
    lane = lax.broadcasted_iota(jnp.int32, (1, 128), 1)

    @pl.loop(0, 4)
    def _(q):
        for a in range(2):
            offset, u, v, low = angle_data(offsets, steps, angle_of(q, a))
            ws = window_start(offset, u, v, low, i // 2, j)
            for tile in range(TILES):
                ty, tx = tile // 4, tile % 4
                corner = offset + u * (COLS * j + TILE * tx) + v * (ROWS * i + TILE * ty) + low * (TILE - 1)
                begin = (corner >> 4) - ws
                block = begin >> 7
                shift = begin & 127
                back = (128 - shift) & 127
                after = jnp.minimum(block + 1, 2)
                left = part[q, pl.ds(4 * a, 4), block].reshape(SLICES, 128)
                right = part[q, pl.ds(4 * a, 4), after].reshape(SLICES, 128)
                left = pltpu.roll(left, back, 1)
                right = pltpu.roll(right, back, 1)
                band = jnp.where(lane < 128 - shift, left, right)
                lhs[q, pl.ds(tile * SLICES, SLICES), pl.ds(128 * a, 128)] = band


def store_picture(acc, out):
    lane = lax.broadcasted_iota(jnp.int32, (1, 128), 1)
    scale = jnp.float32(2.0 / math.sqrt(ANGLES))
    near = lane < 64
    even = (lane & 32) == 0

    @pl.loop(0, 8)
    def _(g):
        at = pl.ds(pl.multiple_of(g * 128, 128), 128)
        for ty in range(2):
            v = [
                (acc[pl.ds((ty * 4 + tx) * SLICES, SLICES), at] * scale).astype(jnp.bfloat16) for tx in range(4)
            ]
            for t in range(2):
                p, q = v[t], v[t + 2]
                v[t] = jnp.where(near, p, pltpu.roll(q, 64, 1))
                v[t + 2] = jnp.where(near, pltpu.roll(p, 64, 1), q)
            for t in (0, 2):
                p, q = v[t], v[t + 1]
                v[t] = jnp.where(even, p, pltpu.roll(q, 32, 1))
                v[t + 1] = jnp.where(even, pltpu.roll(p, 96, 1), q)
            for q in range(4):
                out[TILE * ty + 4 * g + q] = v[q]


def whole_kernel(
    offsets,
    steps,
    sino,
    out,
    rows,
    packed,
    own_a,
    own_b,
    sib_a,
    sib_b,
    ramp_hi,
    ramp_fine,
    filt_acc,
    filt,
    weights,
    lhs,
    acc,
    local_sem,
    row_send,
    row_recv,
    win_send,
    win_recv,
    sib_send,
    sib_recv,
):
    i = lax.axis_index("ang")
    j = lax.axis_index("img")
    core = lax.rem(i, 2)
    row = i // 2

    def partner(k):
        return lax.rem(row + k // IMGD, IMGD), lax.rem(j + lax.rem(k, IMGD), IMGD)

    barrier = pltpu.get_barrier_semaphore()
    own_rows = pltpu.make_async_copy(sino.at[j], rows.at[j], local_sem)
    own_rows.start()

    @pl.loop(1, CHIPS)
    def _(k):
        r, c = partner(k)
        pl.semaphore_signal(barrier, inc=1, device_id=(2 * r + core, c), device_id_type=MESH)

    sibling = (i + 1 - 2 * core, j)
    pl.semaphore_signal(barrier, inc=1, device_id=sibling, device_id_type=MESH)

    ramp_tiles(ramp_hi, ramp_fine)
    pl.semaphore_wait(barrier, CHIPS)

    def row_copy(k):
        to = lax.rem(j + k, IMGD)
        return pltpu.make_async_remote_copy(
            src_ref=sino.at[to],
            dst_ref=rows.at[j],
            send_sem=row_send.at[k],
            recv_sem=row_recv.at[k],
            device_id=(i, to),
            device_id_type=MESH,
        )

    row_copies = [row_copy(k) for k in range(1, IMGD)]
    for c in row_copies:
        c.start()

    def source_angle(q, a, stage):
        back, whose = stage // 2, stage % 2
        chip = lax.rem(row - (q + 4 * back) + IMGD, IMGD)
        side = core if whose == 0 else 1 - core
        return 4 * chip + 2 * side + a

    pixel = lax.broadcasted_iota(jnp.int32, (1, TILE * TILE), 1)
    px = (pixel & (TILE - 1)).astype(jnp.float32) * 0.0625
    py = (pixel >> 5).astype(jnp.float32) * 0.0625
    slot = lax.broadcasted_iota(jnp.int32, (128, TILE * TILE), 0).astype(jnp.float32)
    for stage in range(4):

        @pl.loop(0, 4)
        def _(q):
            for a in range(2):
                offset, u, v, low = angle_data(offsets, steps, source_angle(q, a, stage))
                first = ((offset + low * (TILE - 1)) & 15) - low * (TILE - 1)
                where = (
                    first.astype(jnp.float32) * 0.0625 + u.astype(jnp.float32) * px + v.astype(jnp.float32) * py
                )
                weights[stage, q, pl.ds(128 * a, 128)] = jnp.maximum(1.0 - jnp.abs(slot - where), 0.0).astype(
                    jnp.bfloat16
                )

    own_rows.wait()
    for c in row_copies:
        c.wait()
    filter_rows(rows, filt_acc, filt, ramp_hi, ramp_fine)

    offset, u, v, low = angle_data(offsets, steps, 2 * i + j // 4)
    lane = lax.broadcasted_iota(jnp.int32, (1, 128), 1)

    def pack(k):
        r, c = partner(k)
        ws = window_start(offset, u, v, low, r, c)
        shift = ws & 127
        back = (128 - shift) & 127
        blocks = filt[pl.ds(ws >> 7, 4)]
        rolled = [pltpu.roll(blocks[n], back, 1) for n in range(4)]
        return [jnp.where(lane < 128 - shift, rolled[n], rolled[n + 1]) for n in range(3)]

    def window_copy(k, own, back):
        r, c = partner(k)
        return pltpu.make_async_remote_copy(
            src_ref=packed.at[k],
            dst_ref=own.at[k // IMGD - 4 * back, j],
            send_sem=win_send.at[k],
            recv_sem=win_recv.at[k],
            device_id=(2 * r + core, c),
            device_id_type=MESH,
        )

    def send(ks, own, back):
        for k in ks:
            for n, block in enumerate(pack(k)):
                packed[k, n] = block
        for k in ks:
            window_copy(k, own, back).start()

    for n, block in enumerate(pack(0)):
        own_a[0, j, n] = block
    send([1, 2, 3], own_a, 0)

    @pl.loop(1, 32 // PACK)
    def _(t):
        send([PACK * t + n for n in range(PACK)], own_a, 0)

    @pl.loop(32 // PACK, 64 // PACK)
    def _(t):
        send([PACK * t + n for n in range(PACK)], own_b, 1)

    def share_copy(own, sib, back):
        return pltpu.make_async_remote_copy(
            src_ref=own,
            dst_ref=sib,
            send_sem=sib_send.at[back],
            recv_sem=sib_recv.at[back],
            device_id=sibling,
            device_id_type=MESH,
        )

    def project(stage, part):
        place_lhs(part, lhs, offsets, steps, lambda q, a: source_angle(q, a, stage))
        left = jnp.concatenate([lhs[q] for q in range(4)], axis=1)
        right = weights[stage].reshape(4 * 256, TILE * TILE)
        total = jnp.dot(left, right, preferred_element_type=jnp.float32)
        if stage == 0:
            acc[...] = total
        else:
            acc[...] += total

    @pl.loop(1, 32)
    def _(k):
        window_copy(k, own_a, 0).wait_recv()

    share_a = share_copy(own_a, sib_a, 0)
    share_a.start()
    project(0, own_a)

    @pl.loop(32, 64)
    def _(k):
        window_copy(k, own_b, 1).wait_recv()

    share_b = share_copy(own_b, sib_b, 1)
    share_b.start()
    share_a.wait_recv()
    project(1, sib_a)
    project(2, own_b)
    share_b.wait_recv()
    project(3, sib_b)
    store_picture(acc, out)
    share_a.wait_send()
    share_b.wait_send()

    @pl.loop(1, 32)
    def _(k):
        window_copy(k, own_a, 0).wait_send()

    @pl.loop(32, 64)
    def _(k):
        window_copy(k, own_b, 1).wait_send()


def shards(sinogram, offsets, steps):
    vmem = pl.BlockSpec(memory_space=pltpu.VMEM)
    smem = pl.BlockSpec(memory_space=pltpu.SMEM)
    window = (3, GROUP, 128)
    return pl.pallas_call(
        whole_kernel,
        out_shape=jax.ShapeDtypeStruct((ROWS, SLICES, COLS), jnp.bfloat16),
        in_specs=[smem, smem, vmem],
        out_specs=vmem,
        scratch_shapes=[
            pltpu.VMEM((IMGD, GROUP, BINS // IMGD), jnp.bfloat16),
            pltpu.VMEM((CHIPS, *window), jnp.bfloat16),
            pltpu.VMEM((4, IMGD, *window), jnp.bfloat16),
            pltpu.VMEM((4, IMGD, *window), jnp.bfloat16),
            pltpu.VMEM((4, IMGD, *window), jnp.bfloat16),
            pltpu.VMEM((4, IMGD, *window), jnp.bfloat16),
            pltpu.VMEM((64, 128, 128), jnp.bfloat16),
            pltpu.VMEM((2, 7, 128, 128), jnp.bfloat16),
            pltpu.VMEM((16, GROUP, 256), jnp.float32),
            pltpu.VMEM((36, GROUP, 128), jnp.bfloat16),
            pltpu.VMEM((4, 4, 256, TILE * TILE), jnp.bfloat16),
            pltpu.VMEM((4, TILES * SLICES, 256), jnp.bfloat16),
            pltpu.VMEM((TILES * SLICES, TILE * TILE), jnp.float32),
            pltpu.SemaphoreType.DMA,
            pltpu.SemaphoreType.DMA((IMGD,)),
            pltpu.SemaphoreType.DMA((IMGD,)),
            pltpu.SemaphoreType.DMA((CHIPS,)),
            pltpu.SemaphoreType.DMA((CHIPS,)),
            pltpu.SemaphoreType.DMA((2,)),
            pltpu.SemaphoreType.DMA((2,)),
        ],
        compiler_params=pltpu.CompilerParams(collective_id=0, has_side_effects=True, vmem_limit_bytes=LIMIT),
        name="back_projection",
    )(offsets, steps.T, sinogram.reshape(IMGD, GROUP, BINS // IMGD))


def solution(mesh):
    return jax.shard_map(
        shards,
        mesh=mesh,
        in_specs=(P("ang", None, "img"), P(), P()),
        out_specs=P("ang", None, "img"),
        check_vma=False,
    )
```

```python
import math

import jax
import jax.numpy as jnp
from jax import lax
from jax.experimental import pallas as pl
from jax.experimental.pallas import tpu as pltpu
from jax.sharding import PartitionSpec as P

BINS = 4096
IMG = 1024
ANGLES = 32
SLICES = 64
ANG = 16
IMGD = 8
ROWS = IMG // ANG
COLS = IMG // IMGD
TILE = 32
TILES = 8
GROUP = 16
MESH = pl.DeviceIdType.MESH
LIMIT = 48 * 1024 * 1024


def ramp_tiles(ramp_hi, ramp_fine):
    gap = lax.broadcasted_iota(jnp.int32, (128, 128), 1) - lax.broadcasted_iota(jnp.int32, (128, 128), 0)
    scale = jnp.where((gap & 1) != 0, jnp.float32(-1.0 / math.pi**2), jnp.float32(0.0))
    gap_f = gap.astype(jnp.float32)

    def value(e):
        t = gap_f + jnp.asarray(128 * e).astype(jnp.float32)
        t = jnp.where(t == 0.0, jnp.float32(1.0), t)
        return scale / (t * t)

    @pl.loop(0, 64)
    def _(e):
        ramp_hi[e] = value(e - 32).astype(jnp.bfloat16)

    for e in range(-3, 4):
        v = value(e)
        if e == 0:
            v = jnp.where(gap == 0, jnp.float32(0.25), v)
        hi = v.astype(jnp.bfloat16)
        rest = v - hi.astype(jnp.float32)
        mid = rest.astype(jnp.bfloat16)
        low = (rest - mid.astype(jnp.float32)).astype(jnp.bfloat16)
        ramp_hi[e + 32] = hi
        ramp_fine[0, e + 3] = mid
        ramp_fine[1, e + 3] = low


def toeplitz(tiles, at):
    top = jnp.concatenate([tiles[at], tiles[at + 1]], axis=1)
    low = jnp.concatenate([tiles[at - 1], tiles[at]], axis=1)
    return jnp.concatenate([top, low], axis=0)


def filter_rows(rows, acc, filt, ramp_hi, ramp_fine):
    for d in sorted(range(-15, 16), key=abs):
        count = 16 - abs(d)
        first = max(0, -d)
        lhs = jnp.concatenate(
            [rows[b // 2, :, pl.ds(256 * (b % 2), 256)] for b in range(first, first + count)], axis=0
        )
        total = jnp.dot(lhs, toeplitz(ramp_hi, 2 * d + 32), preferred_element_type=jnp.float32)
        if abs(d) <= 1:
            for term in range(2):
                total += jnp.dot(
                    lhs, toeplitz(ramp_fine.at[term], 2 * d + 3), preferred_element_type=jnp.float32
                )
        total = total.reshape(count, GROUP, 256)
        if d == 0:
            acc[...] = total
        else:
            acc[pl.ds(max(0, d), count)] += total
    for b in range(16):
        for h in range(2):
            filt[2 * b + h] = acc[b, :, pl.ds(128 * h, 128)].astype(jnp.bfloat16)
    filt[pl.ds(32, 4)] = jnp.zeros((4, GROUP, 128), jnp.bfloat16)


def angle_data(offsets, steps, a):
    u = steps[0, a]
    v = steps[1, a]
    return offsets[a], u, v, jnp.minimum(u, 0) + jnp.minimum(v, 0)


def window_start(offset, u, v, low, chip_row, img):
    return (offset + u * (COLS * img) + v * (2 * ROWS * chip_row) + low * 127) >> 4


def place_lhs(part, lhs, offsets, steps, angle_of):
    i = lax.axis_index("ang")
    j = lax.axis_index("img")
    lane = lax.broadcasted_iota(jnp.int32, (1, 128), 1)
    for q in range(2):
        for a in range(2):
            offset, u, v, low = angle_data(offsets, steps, angle_of(q, a))
            ws = window_start(offset, u, v, low, i >> 1, j)
            base = offset + u * (COLS * j) + v * (ROWS * i) + low * (TILE - 1)
            for tile in range(TILES):
                ty, tx = tile // 4, tile % 4
                begin = ((base + u * (TILE * tx) + v * (TILE * ty)) >> 4) - ws
                block = begin >> 7
                shift = begin & 127
                back = (128 - shift) & 127
                after = jnp.minimum(block + 1, 2)
                left = part[q, pl.ds(4 * a, 4), block].reshape(SLICES, 128)
                right = part[q, pl.ds(4 * a, 4), after].reshape(SLICES, 128)
                left = pltpu.roll(left, back, 1)
                right = pltpu.roll(right, back, 1)
                band = jnp.where(lane < 128 - shift, left, right)
                lhs[pl.ds(tile * SLICES, SLICES), pl.ds(256 * q + 128 * a, 128)] = band


def store_picture(acc, out):
    lane = lax.broadcasted_iota(jnp.int32, (1, 128), 1)
    scale = jnp.float32(2.0 / math.sqrt(ANGLES))
    near = lane < 64
    even = (lane & 32) == 0

    @pl.loop(0, 8)
    def _(g):
        at = pl.ds(pl.multiple_of(g * 128, 128), 128)
        for ty in range(2):
            v = [
                (acc[pl.ds((ty * 4 + tx) * SLICES, SLICES), at] * scale).astype(jnp.bfloat16) for tx in range(4)
            ]
            for t in range(2):
                p, q = v[t], v[t + 2]
                v[t] = jnp.where(near, p, pltpu.roll(q, 64, 1))
                v[t + 2] = jnp.where(near, pltpu.roll(p, 64, 1), q)
            for t in (0, 2):
                p, q = v[t], v[t + 1]
                v[t] = jnp.where(even, p, pltpu.roll(q, 32, 1))
                v[t + 1] = jnp.where(even, pltpu.roll(p, 96, 1), q)
            for q in range(4):
                out[TILE * ty + 4 * g + q] = v[q]


def whole_kernel(
    offsets_in,
    steps_in,
    sino,
    out,
    offsets,
    steps,
    rows,
    packed,
    own_0,
    own_1,
    own_2,
    own_3,
    sib_0,
    sib_1,
    sib_2,
    sib_3,
    ramp_hi,
    ramp_fine,
    filt_acc,
    filt,
    weights,
    lhs_0,
    lhs_1,
    acc,
    local_sem,
    row_send,
    row_recv,
    win_send,
    win_recv,
    sib_send,
    sib_recv,
):
    i = lax.axis_index("ang")
    j = lax.axis_index("img")
    core = i & 1
    row = i >> 1
    sibling = (i + 1 - 2 * core, j)
    own = (own_0, own_1, own_2, own_3)
    sib = (sib_0, sib_1, sib_2, sib_3)

    barrier = pltpu.get_barrier_semaphore()
    for k in range(1, IMGD):
        pl.semaphore_signal(barrier, inc=1, device_id=(i, (j + k) & 7), device_id_type=MESH)
    for k in range(1, IMGD):
        pl.semaphore_signal(barrier, inc=1, device_id=((i + 2 * k) & 15, j), device_id_type=MESH)
    pl.semaphore_signal(barrier, inc=1, device_id=sibling, device_id_type=MESH)
    local = [
        pltpu.make_async_copy(offsets_in, offsets, local_sem.at[0]),
        pltpu.make_async_copy(steps_in, steps, local_sem.at[1]),
        pltpu.make_async_copy(sino.at[j], rows.at[j], local_sem.at[2]),
    ]
    for c in local:
        c.start()
    pl.semaphore_wait(barrier, 15)

    def row_copy(k):
        to = (j + k) & 7
        return pltpu.make_async_remote_copy(
            src_ref=sino.at[to],
            dst_ref=rows.at[j],
            send_sem=row_send.at[k],
            recv_sem=row_recv.at[k],
            device_id=(i, to),
            device_id_type=MESH,
        )

    row_copies = [row_copy(k) for k in range(1, IMGD)]
    for c in row_copies:
        c.start()
    for c in local:
        c.wait()
    ramp_tiles(ramp_hi, ramp_fine)

    def source_angle(stage, q, a):
        chip = (row - (2 * (stage >> 1) + q)) & 7
        side = core ^ (stage & 1)
        return 4 * chip + 2 * side + a

    pixel = lax.broadcasted_iota(jnp.int32, (1, TILE * TILE), 1)
    px = (pixel & (TILE - 1)).astype(jnp.float32) * 0.0625
    py = (pixel >> 5).astype(jnp.float32) * 0.0625
    slot = lax.broadcasted_iota(jnp.int32, (128, TILE * TILE), 0).astype(jnp.float32)

    @pl.loop(0, 8)
    def _(stage):
        for q in range(2):
            for a in range(2):
                offset, u, v, low = angle_data(offsets, steps, source_angle(stage, q, a))
                first = ((offset + low * (TILE - 1)) & 15) - low * (TILE - 1)
                where = (
                    first.astype(jnp.float32) * 0.0625 + u.astype(jnp.float32) * px + v.astype(jnp.float32) * py
                )
                weights[stage, pl.ds(256 * q + 128 * a, 128)] = jnp.maximum(
                    1.0 - jnp.abs(slot - where), 0.0
                ).astype(jnp.bfloat16)

    for c in row_copies:
        c.wait_recv()
    filter_rows(rows, filt_acc, filt, ramp_hi, ramp_fine)

    offset, u, v, low = angle_data(offsets, steps, 2 * i + (j >> 2))
    lane = lax.broadcasted_iota(jnp.int32, (1, 128), 1)

    def pack(r, c):
        ws = window_start(offset, u, v, low, r, c)
        shift = ws & 127
        back = (128 - shift) & 127
        blocks = filt[pl.ds(ws >> 7, 4)]
        rolled = [pltpu.roll(blocks[n], back, 1) for n in range(4)]
        return [jnp.where(lane < 128 - shift, rolled[n], rolled[n + 1]) for n in range(3)]

    def window_copy(group, k, part, q):
        r = (row + group) & 7
        c = (j + k) & 7
        return pltpu.make_async_remote_copy(
            src_ref=packed.at[group, k],
            dst_ref=part.at[q, j],
            send_sem=win_send.at[group],
            recv_sem=win_recv.at[group],
            device_id=(2 * r + core, c),
            device_id_type=MESH,
        )

    def group_copy(group, part, q, count):
        return pltpu.make_async_remote_copy(
            src_ref=packed.at[group, pl.ds(IMGD - count, count)],
            dst_ref=part.at[q, pl.ds(0, count)],
            send_sem=win_send.at[group],
            recv_sem=win_recv.at[group],
            device_id=sibling,
            device_id_type=MESH,
        )

    for n, block in enumerate(pack(row, j)):
        own_0[0, j, n] = block
    for group in range(8):
        r = (row + group) & 7
        ks = range(1 if group == 0 else 0, IMGD)
        for half in (ks[: len(ks) // 2], ks[len(ks) // 2 :]):
            for k in half:
                for n, block in enumerate(pack(r, (j + k) & 7)):
                    packed[group, k, n] = block
            for k in half:
                window_copy(group, k, own[group // 2], group % 2).start()

    def group_waits(p):
        return [group_copy(2 * p + q, own[p], q, 7 if 2 * p + q == 0 else 8) for q in range(2)]

    def share_copy(p):
        return pltpu.make_async_remote_copy(
            src_ref=own[p],
            dst_ref=sib[p],
            send_sem=sib_send.at[p],
            recv_sem=sib_recv.at[p],
            device_id=sibling,
            device_id_type=MESH,
        )

    def arrive(p):
        for c in group_waits(p):
            c.wait_recv()
        share_copy(p).start()

    def prepare(stage, n):
        p = stage // 2
        place_lhs(
            (own if stage % 2 == 0 else sib)[p],
            (lhs_0, lhs_1)[n % 2],
            offsets,
            steps,
            lambda q, a: source_angle(stage, q, a),
        )

    order = (0, 2, 1, 4, 3, 6, 5, 7)
    arrive(0)
    prepare(0, 0)
    for n, stage in enumerate(order):
        if n + 1 < 8:
            after = order[n + 1]
            if after in (2, 4, 6):
                arrive(after // 2)
            if after % 2 == 1:
                share_copy(after // 2).wait_recv()
            prepare(after, n + 1)
        total = jnp.dot((lhs_0, lhs_1)[n % 2][...], weights[stage], preferred_element_type=jnp.float32)
        if n == 0:
            acc[...] = total
        else:
            acc[...] += total
    store_picture(acc, out)
    for c in row_copies:
        c.wait_send()
    for p in range(4):
        share_copy(p).wait_send()
        for c in group_waits(p):
            c.wait_send()


def shards(sinogram, offsets, steps):
    vmem = pl.BlockSpec(memory_space=pltpu.VMEM)
    hbm = pl.BlockSpec(memory_space=pl.ANY)
    window = (3, GROUP, 128)
    return pl.pallas_call(
        whole_kernel,
        out_shape=jax.ShapeDtypeStruct((ROWS, SLICES, COLS), jnp.bfloat16),
        in_specs=[hbm, hbm, hbm],
        out_specs=vmem,
        scratch_shapes=[
            pltpu.SMEM((ANGLES,), jnp.int32),
            pltpu.SMEM((2, ANGLES), jnp.int32),
            pltpu.VMEM((IMGD, GROUP, BINS // IMGD), jnp.bfloat16),
            pltpu.VMEM((8, IMGD, *window), jnp.bfloat16),
            *([pltpu.VMEM((2, IMGD, *window), jnp.bfloat16)] * 8),
            pltpu.VMEM((64, 128, 128), jnp.bfloat16),
            pltpu.VMEM((2, 7, 128, 128), jnp.bfloat16),
            pltpu.VMEM((16, GROUP, 256), jnp.float32),
            pltpu.VMEM((36, GROUP, 128), jnp.bfloat16),
            pltpu.VMEM((8, 512, TILE * TILE), jnp.bfloat16),
            pltpu.VMEM((TILES * SLICES, 512), jnp.bfloat16),
            pltpu.VMEM((TILES * SLICES, 512), jnp.bfloat16),
            pltpu.VMEM((TILES * SLICES, TILE * TILE), jnp.float32),
            pltpu.SemaphoreType.DMA((3,)),
            pltpu.SemaphoreType.DMA((IMGD,)),
            pltpu.SemaphoreType.DMA((IMGD,)),
            pltpu.SemaphoreType.DMA((8,)),
            pltpu.SemaphoreType.DMA((8,)),
            pltpu.SemaphoreType.DMA((4,)),
            pltpu.SemaphoreType.DMA((4,)),
        ],
        compiler_params=pltpu.CompilerParams(collective_id=0, has_side_effects=True, vmem_limit_bytes=LIMIT),
        name="back_projection",
    )(offsets, steps.T, sinogram.reshape(IMGD, GROUP, BINS // IMGD))


def solution(mesh):
    return jax.shard_map(
        shards,
        mesh=mesh,
        in_specs=(P("ang", None, "img"), P(), P()),
        out_specs=P("ang", None, "img"),
        check_vma=False,
    )
```

```python
import math

import jax
import jax.numpy as jnp
from jax import lax
from jax.experimental import pallas as pl
from jax.experimental.pallas import tpu as pltpu
from jax.sharding import PartitionSpec as P

BINS = 4096
IMG = 1024
ANGLES = 32
SLICES = 64
ANG = 16
IMGD = 8
ROWS = IMG // ANG
COLS = IMG // IMGD
TILE = 32
TILES = 8
GROUP = 16
MESH = pl.DeviceIdType.MESH
LIMIT = 48 * 1024 * 1024


def ramp_tiles(ramp_hi, ramp_fine):
    gap = lax.broadcasted_iota(jnp.int32, (128, 128), 1) - lax.broadcasted_iota(jnp.int32, (128, 128), 0)
    scale = jnp.where((gap & 1) != 0, jnp.float32(-1.0 / math.pi**2), jnp.float32(0.0))
    gap_f = gap.astype(jnp.float32)

    def value(e):
        t = gap_f + jnp.asarray(128 * e).astype(jnp.float32)
        t = jnp.where(t == 0.0, jnp.float32(1.0), t)
        return scale / (t * t)

    @pl.loop(0, 64)
    def _(e):
        ramp_hi[e] = value(e - 32).astype(jnp.bfloat16)

    for e in range(-3, 4):
        v = value(e)
        if e == 0:
            v = jnp.where(gap == 0, jnp.float32(0.25), v)
        hi = v.astype(jnp.bfloat16)
        rest = v - hi.astype(jnp.float32)
        mid = rest.astype(jnp.bfloat16)
        low = (rest - mid.astype(jnp.float32)).astype(jnp.bfloat16)
        ramp_hi[e + 32] = hi
        ramp_fine[0, e + 3] = mid
        ramp_fine[1, e + 3] = low


def toeplitz(tiles, at):
    top = jnp.concatenate([tiles[at], tiles[at + 1]], axis=1)
    low = jnp.concatenate([tiles[at - 1], tiles[at]], axis=1)
    return jnp.concatenate([top, low], axis=0)


def filter_rows(rows, acc, filt, ramp_hi, ramp_fine):
    for d in sorted(range(-15, 16), key=abs):
        count = 16 - abs(d)
        first = max(0, -d)
        lhs = jnp.concatenate(
            [rows[b // 2, :, pl.ds(256 * (b % 2), 256)] for b in range(first, first + count)], axis=0
        )
        total = jnp.dot(lhs, toeplitz(ramp_hi, 2 * d + 32), preferred_element_type=jnp.float32)
        if abs(d) <= 1:
            for term in range(2):
                total += jnp.dot(
                    lhs, toeplitz(ramp_fine.at[term], 2 * d + 3), preferred_element_type=jnp.float32
                )
        total = total.reshape(count, GROUP, 256)
        if d == 0:
            acc[...] = total
        else:
            acc[pl.ds(max(0, d), count)] += total
    for b in range(16):
        for h in range(2):
            filt[2 * b + h] = acc[b, :, pl.ds(128 * h, 128)].astype(jnp.bfloat16)
    filt[pl.ds(32, 4)] = jnp.zeros((4, GROUP, 128), jnp.bfloat16)


def angle_data(offsets, steps, a):
    u = steps[0, a]
    v = steps[1, a]
    return offsets[a], u, v, jnp.minimum(u, 0) + jnp.minimum(v, 0)


def window_start(offset, u, v, low, chip_row, img):
    return (offset + u * (COLS * img) + v * (2 * ROWS * chip_row) + low * 127) >> 4


def place_lhs(part, lhs, offsets, steps, angle_of):
    i = lax.axis_index("ang")
    j = lax.axis_index("img")
    lane = lax.broadcasted_iota(jnp.int32, (1, 128), 1)
    for dx in range(4):
        offset, u, v, low = angle_data(offsets, steps, angle_of(dx))
        ws = window_start(offset, u, v, low, i >> 1, j)
        base = offset + u * (COLS * j) + v * (ROWS * i) + low * (TILE - 1)
        for tile in range(TILES):
            ty, tx = tile // 4, tile % 4
            begin = ((base + u * (TILE * tx) + v * (TILE * ty)) >> 4) - ws
            block = begin >> 7
            shift = begin & 127
            back = (128 - shift) & 127
            after = jnp.minimum(block + 1, 2)
            left = part[pl.ds(4 * dx, 4), block].reshape(SLICES, 128)
            right = part[pl.ds(4 * dx, 4), after].reshape(SLICES, 128)
            left = pltpu.roll(left, back, 1)
            right = pltpu.roll(right, back, 1)
            band = jnp.where(lane < 128 - shift, left, right)
            lhs[pl.ds(tile * SLICES, SLICES), pl.ds(128 * dx, 128)] = band


def store_rows(values, out, first):
    lane = lax.broadcasted_iota(jnp.int32, (1, 128), 1)
    scale = jnp.float32(2.0 / math.sqrt(ANGLES))
    near = lane < 64
    even = (lane & 32) == 0
    values = (values * scale).astype(jnp.bfloat16)
    for g in range(values.shape[1] // 128):
        for ty in range(2):
            v = [
                values[(ty * 4 + tx) * SLICES : (ty * 4 + tx + 1) * SLICES, g * 128 : g * 128 + 128]
                for tx in range(4)
            ]
            for t in range(2):
                p, q = v[t], v[t + 2]
                v[t] = jnp.where(near, p, pltpu.roll(q, 64, 1))
                v[t + 2] = jnp.where(near, pltpu.roll(p, 64, 1), q)
            for t in (0, 2):
                p, q = v[t], v[t + 1]
                v[t] = jnp.where(even, p, pltpu.roll(q, 32, 1))
                v[t + 1] = jnp.where(even, pltpu.roll(p, 96, 1), q)
            for q in range(4):
                out[TILE * ty + first + 4 * g + q] = v[q]


def whole_kernel(
    offsets_in,
    steps_in,
    sino,
    out,
    offsets,
    steps,
    rows,
    packed,
    own_0,
    own_1,
    own_2,
    own_3,
    sib_0,
    sib_1,
    sib_2,
    sib_3,
    ramp_hi,
    ramp_fine,
    filt_acc,
    filt,
    weights,
    lhs_0,
    lhs_1,
    acc,
    local_sem,
    row_send,
    row_recv,
    win_send,
    win_recv,
    sib_send,
    sib_recv,
):
    i = lax.axis_index("ang")
    j = lax.axis_index("img")
    core = i & 1
    row = i >> 1
    x, y, z = row & 3, j & 3, 2 * (j >> 2) + (row >> 2)
    sibling = (i + 1 - 2 * core, j)
    own = (own_0, own_1, own_2, own_3)
    sib = (sib_0, sib_1, sib_2, sib_3)

    barrier = pltpu.get_barrier_semaphore()
    for k in range(1, IMGD):
        pl.semaphore_signal(barrier, inc=1, device_id=(i, (j + k) & 7), device_id_type=MESH)
    for k in range(1, IMGD):
        pl.semaphore_signal(barrier, inc=1, device_id=((i + 2 * k) & 15, j), device_id_type=MESH)
    pl.semaphore_signal(barrier, inc=1, device_id=sibling, device_id_type=MESH)
    local = [
        pltpu.make_async_copy(offsets_in, offsets, local_sem.at[0]),
        pltpu.make_async_copy(steps_in, steps, local_sem.at[1]),
        pltpu.make_async_copy(sino.at[j], rows.at[j], local_sem.at[2]),
    ]
    for c in local:
        c.start()
    pl.semaphore_wait(barrier, 15)

    def row_copy(k):
        to = (j + k) & 7
        return pltpu.make_async_remote_copy(
            src_ref=sino.at[to],
            dst_ref=rows.at[j],
            send_sem=row_send.at[k],
            recv_sem=row_recv.at[k],
            device_id=(i, to),
            device_id_type=MESH,
        )

    row_copies = [row_copy(k) for k in range(1, IMGD)]
    for c in row_copies:
        c.start()
    for c in local:
        c.wait()
    ramp_tiles(ramp_hi, ramp_fine)

    for c in row_copies:
        c.wait_recv()
    filter_rows(rows, filt_acc, filt, ramp_hi, ramp_fine)

    offset, u, v, low = angle_data(offsets, steps, 2 * i + (j >> 2))
    lane = lax.broadcasted_iota(jnp.int32, (1, 128), 1)

    def pack(r, c):
        ws = window_start(offset, u, v, low, r, c)
        shift = ws & 127
        back = (128 - shift) & 127
        blocks = filt[pl.ds(ws >> 7, 4)]
        rolled = [pltpu.roll(blocks[n], back, 1) for n in range(4)]
        return [jnp.where(lane < 128 - shift, rolled[n], rolled[n + 1]) for n in range(3)]

    def partner(p, dx, dy):
        xt, yt, zt = (x + dx) & 3, (y + dy) & 3, (z + dx + p) & 3
        return 4 * (zt & 1) + xt, 4 * (zt >> 1) + yt

    def window_copy(p, dx, dy):
        r, c = partner(p, dx, dy)
        return pltpu.make_async_remote_copy(
            src_ref=packed.at[p, 4 * dx + dy],
            dst_ref=own[p].at[4 * dx + y],
            send_sem=win_send.at[p],
            recv_sem=win_recv.at[p],
            device_id=(2 * r + core, c),
            device_id_type=MESH,
        )

    def stage_copy(p):
        count = 15 if p == 0 else 16
        return pltpu.make_async_remote_copy(
            src_ref=packed.at[p, pl.ds(16 - count, count)],
            dst_ref=own[p].at[pl.ds(0, count)],
            send_sem=win_send.at[p],
            recv_sem=win_recv.at[p],
            device_id=sibling,
            device_id_type=MESH,
        )

    for p in range(4):
        for dy in range(4):
            for dx in range(4):
                mine = p == 0 and dx == 0 and dy == 0
                for n, block in enumerate(pack(*partner(p, dx, dy))):
                    if mine:
                        own_0[y, n] = block
                    else:
                        packed[p, 4 * dx + dy, n] = block
            for dx in range(4):
                if p + dx + dy > 0:
                    window_copy(p, dx, dy).start()

    def source_angle(p, side, dx):
        xs, zs = (x - dx) & 3, (z - dx - p) & 3
        return 4 * (4 * (zs & 1) + xs) + 2 * (core ^ side) + (zs >> 1)

    pixel = lax.broadcasted_iota(jnp.int32, (1, TILE * TILE), 1)
    px = (pixel & (TILE - 1)).astype(jnp.float32) * 0.0625
    py = (pixel >> 5).astype(jnp.float32) * 0.0625
    slot = lax.broadcasted_iota(jnp.int32, (128, TILE * TILE), 0).astype(jnp.float32)

    @pl.loop(0, 8)
    def _(stage):
        for dx in range(4):
            offset, u, v, low = angle_data(offsets, steps, source_angle(stage >> 1, stage & 1, dx))
            first = ((offset + low * (TILE - 1)) & 15) - low * (TILE - 1)
            where = first.astype(jnp.float32) * 0.0625 + u.astype(jnp.float32) * px + v.astype(jnp.float32) * py
            weights[stage, pl.ds(128 * dx, 128)] = jnp.maximum(1.0 - jnp.abs(slot - where), 0.0).astype(jnp.bfloat16)

    def share_copy(p):
        return pltpu.make_async_remote_copy(
            src_ref=own[p],
            dst_ref=sib[p],
            send_sem=sib_send.at[p],
            recv_sem=sib_recv.at[p],
            device_id=sibling,
            device_id_type=MESH,
        )

    def arrive(p):
        stage_copy(p).wait_recv()
        share_copy(p).start()

    def prepare(stage, n):
        p, side = stage // 2, stage % 2
        place_lhs((own, sib)[side][p], (lhs_0, lhs_1)[n % 2], offsets, steps, lambda dx: source_angle(p, side, dx))

    order = (0, 2, 1, 4, 3, 6, 5, 7)
    arrive(0)
    prepare(0, 0)
    for n, stage in enumerate(order[:-1]):
        after = order[n + 1]
        if after in (2, 4, 6):
            arrive(after // 2)
        if after % 2 == 1:
            share_copy(after // 2).wait_recv()
        prepare(after, n + 1)
        total = jnp.dot((lhs_0, lhs_1)[n % 2][...], weights[stage], preferred_element_type=jnp.float32)
        if n == 0:
            acc[...] = total
        else:
            acc[...] += total
    for part in range(4):
        at = pl.ds(256 * part, 256)
        total = acc[:, at] + jnp.dot(lhs_1[...], weights[7, :, at], preferred_element_type=jnp.float32)
        store_rows(total, out, 8 * part)
    for c in row_copies:
        c.wait_send()
    for p in range(4):
        share_copy(p).wait_send()
        stage_copy(p).wait_send()


def shards(sinogram, offsets, steps):
    vmem = pl.BlockSpec(memory_space=pltpu.VMEM)
    hbm = pl.BlockSpec(memory_space=pltpu.HBM)
    window = (3, GROUP, 128)
    return pl.pallas_call(
        whole_kernel,
        out_shape=jax.ShapeDtypeStruct((ROWS, SLICES, COLS), jnp.bfloat16),
        in_specs=[hbm, hbm, hbm],
        out_specs=vmem,
        scratch_shapes=[
            pltpu.SMEM((ANGLES,), jnp.int32),
            pltpu.SMEM((2, ANGLES), jnp.int32),
            pltpu.VMEM((IMGD, GROUP, BINS // IMGD), jnp.bfloat16),
            pltpu.VMEM((4, 16, *window), jnp.bfloat16),
            *([pltpu.VMEM((16, *window), jnp.bfloat16)] * 8),
            pltpu.VMEM((64, 128, 128), jnp.bfloat16),
            pltpu.VMEM((2, 7, 128, 128), jnp.bfloat16),
            pltpu.VMEM((16, GROUP, 256), jnp.float32),
            pltpu.VMEM((36, GROUP, 128), jnp.bfloat16),
            pltpu.VMEM((8, 512, TILE * TILE), jnp.bfloat16),
            pltpu.VMEM((TILES * SLICES, 512), jnp.bfloat16),
            pltpu.VMEM((TILES * SLICES, 512), jnp.bfloat16),
            pltpu.VMEM((TILES * SLICES, TILE * TILE), jnp.float32),
            pltpu.SemaphoreType.DMA((3,)),
            pltpu.SemaphoreType.DMA((IMGD,)),
            pltpu.SemaphoreType.DMA((IMGD,)),
            pltpu.SemaphoreType.DMA((4,)),
            pltpu.SemaphoreType.DMA((4,)),
            pltpu.SemaphoreType.DMA((4,)),
            pltpu.SemaphoreType.DMA((4,)),
        ],
        compiler_params=pltpu.CompilerParams(collective_id=0, has_side_effects=True, vmem_limit_bytes=LIMIT),
        name="back_projection",
    )(offsets, steps.T, sinogram.reshape(IMGD, GROUP, BINS // IMGD))


def solution(mesh):
    return jax.shard_map(
        shards,
        mesh=mesh,
        in_specs=(P("ang", None, "img"), P(), P()),
        out_specs=P("ang", None, "img"),
        check_vma=False,
    )
```

```python
import math

import jax
import jax.numpy as jnp
from jax import lax
from jax.experimental import pallas as pl
from jax.experimental.pallas import tpu as pltpu
from jax.sharding import PartitionSpec as P

BINS = 4096
IMG = 1024
ANGLES = 32
SLICES = 64
ANG = 16
IMGD = 8
ROWS = IMG // ANG
COLS = IMG // IMGD
TILE = 32
TILES = 8
GROUP = 16
MESH = pl.DeviceIdType.MESH
LIMIT = 48 * 1024 * 1024


def ramp_tiles(ramp_hi, ramp_fine):
    gap = lax.broadcasted_iota(jnp.int32, (128, 128), 1) - lax.broadcasted_iota(jnp.int32, (128, 128), 0)
    scale = jnp.where((gap & 1) != 0, jnp.float32(-1.0 / math.pi**2), jnp.float32(0.0))
    gap_f = gap.astype(jnp.float32)

    def value(e):
        t = gap_f + jnp.asarray(128 * e).astype(jnp.float32)
        t = jnp.where(t == 0.0, jnp.float32(1.0), t)
        return scale / (t * t)

    @pl.loop(0, 64)
    def _(e):
        ramp_hi[e] = value(e - 32).astype(jnp.bfloat16)

    for e in range(-3, 4):
        v = value(e)
        if e == 0:
            v = jnp.where(gap == 0, jnp.float32(0.25), v)
        hi = v.astype(jnp.bfloat16)
        rest = v - hi.astype(jnp.float32)
        mid = rest.astype(jnp.bfloat16)
        low = (rest - mid.astype(jnp.float32)).astype(jnp.bfloat16)
        ramp_hi[e + 32] = hi
        ramp_fine[0, e + 3] = mid
        ramp_fine[1, e + 3] = low


def toeplitz(tiles, at):
    top = jnp.concatenate([tiles[at], tiles[at + 1]], axis=1)
    low = jnp.concatenate([tiles[at - 1], tiles[at]], axis=1)
    return jnp.concatenate([top, low], axis=0)


def filter_rows(rows, acc, filt, ramp_hi, ramp_fine):
    for d in sorted(range(-15, 16), key=abs):
        count = 16 - abs(d)
        first = max(0, -d)
        lhs = jnp.concatenate(
            [rows[b // 2, :, pl.ds(256 * (b % 2), 256)] for b in range(first, first + count)], axis=0
        )
        total = jnp.dot(lhs, toeplitz(ramp_hi, 2 * d + 32), preferred_element_type=jnp.float32)
        if abs(d) <= 1:
            for term in range(2):
                total += jnp.dot(
                    lhs, toeplitz(ramp_fine.at[term], 2 * d + 3), preferred_element_type=jnp.float32
                )
        total = total.reshape(count, GROUP, 256)
        if d == 0:
            acc[...] = total
        else:
            acc[pl.ds(max(0, d), count)] += total
    for b in range(16):
        for h in range(2):
            filt[2 * b + h] = acc[b, :, pl.ds(128 * h, 128)].astype(jnp.bfloat16)
    filt[pl.ds(32, 4)] = jnp.zeros((4, GROUP, 128), jnp.bfloat16)


def angle_data(offsets, steps, a):
    u = steps[0, a]
    v = steps[1, a]
    return offsets[a], u, v, jnp.minimum(u, 0) + jnp.minimum(v, 0)


def window_start(offset, u, v, low, chip_row, img):
    return (offset + u * (COLS * img) + v * (2 * ROWS * chip_row) + low * 127) >> 4


def place_lhs(windows, p, lhs, offsets, steps, angle_of):
    i = lax.axis_index("ang")
    j = lax.axis_index("img")
    lane = lax.broadcasted_iota(jnp.int32, (1, 128), 1)
    for dx in range(4):
        offset, u, v, low = angle_data(offsets, steps, angle_of(dx))
        ws = window_start(offset, u, v, low, i >> 1, j)
        base = offset + u * (COLS * j) + v * (ROWS * i) + low * (TILE - 1)
        blocks = [windows[p, pl.ds(4 * dx, 4), n].reshape(SLICES, 128) for n in range(3)]
        for tile in range(TILES):
            ty, tx = tile // 4, tile % 4
            begin = ((base + u * (TILE * tx) + v * (TILE * ty)) >> 4) - ws
            back = (128 - (begin & 127)) & 127
            left = jnp.where(begin < 128, blocks[0], jnp.where(begin < 256, blocks[1], blocks[2]))
            right = jnp.where(begin < 128, blocks[1], blocks[2])
            left = pltpu.roll(left, back, 1)
            right = pltpu.roll(right, back, 1)
            band = jnp.where(lane < 128 - (begin & 127), left, right)
            lhs[pl.ds(tile * SLICES, SLICES), pl.ds(128 * dx, 128)] = band


def store_rows(values, out, first):
    lane = lax.broadcasted_iota(jnp.int32, (1, 128), 1)
    scale = jnp.float32(2.0 / math.sqrt(ANGLES))
    near = lane < 64
    even = (lane & 32) == 0
    values = (values * scale).astype(jnp.bfloat16)
    for g in range(values.shape[1] // 128):
        for ty in range(2):
            v = [
                values[(ty * 4 + tx) * SLICES : (ty * 4 + tx + 1) * SLICES, g * 128 : g * 128 + 128]
                for tx in range(4)
            ]
            for t in range(2):
                p, q = v[t], v[t + 2]
                v[t] = jnp.where(near, p, pltpu.roll(q, 64, 1))
                v[t + 2] = jnp.where(near, pltpu.roll(p, 64, 1), q)
            for t in (0, 2):
                p, q = v[t], v[t + 1]
                v[t] = jnp.where(even, p, pltpu.roll(q, 32, 1))
                v[t + 1] = jnp.where(even, pltpu.roll(p, 96, 1), q)
            for q in range(4):
                out[TILE * ty + first + 4 * g + q] = v[q]


def whole_kernel(
    offsets_in,
    steps_in,
    sino,
    out,
    offsets,
    steps,
    rows,
    packed,
    own,
    sib,
    ramp_hi,
    ramp_fine,
    filt_acc,
    filt,
    weights,
    lhs_0,
    lhs_1,
    acc,
    local_sem,
    row_send,
    row_recv,
    win_send,
    win_recv,
    sib_send,
    sib_recv,
):
    i = lax.axis_index("ang")
    j = lax.axis_index("img")
    core = i & 1
    row = i >> 1
    x, y, z = row & 3, j & 3, 2 * (j >> 2) + (row >> 2)
    sibling = (i + 1 - 2 * core, j)

    barrier = pltpu.get_barrier_semaphore()
    for k in range(1, IMGD):
        pl.semaphore_signal(barrier, inc=1, device_id=(i, (j + k) & 7), device_id_type=MESH)
    for k in range(1, IMGD):
        pl.semaphore_signal(barrier, inc=1, device_id=((i + 2 * k) & 15, j), device_id_type=MESH)
    pl.semaphore_signal(barrier, inc=1, device_id=sibling, device_id_type=MESH)
    local = [
        pltpu.make_async_copy(offsets_in, offsets, local_sem.at[0]),
        pltpu.make_async_copy(steps_in, steps, local_sem.at[1]),
        pltpu.make_async_copy(sino.at[j], rows.at[j], local_sem.at[2]),
    ]
    for c in local:
        c.start()
    pl.semaphore_wait(barrier, 15)

    def row_copy(k):
        to = (j + k) & 7
        return pltpu.make_async_remote_copy(
            src_ref=sino.at[to],
            dst_ref=rows.at[j],
            send_sem=row_send.at[k],
            recv_sem=row_recv.at[k],
            device_id=(i, to),
            device_id_type=MESH,
        )

    row_copies = [row_copy(k) for k in range(1, IMGD)]
    for c in row_copies:
        c.start()
    for c in local:
        c.wait()
    ramp_tiles(ramp_hi, ramp_fine)

    for c in row_copies:
        c.wait_recv()
    filter_rows(rows, filt_acc, filt, ramp_hi, ramp_fine)

    offset, u, v, low = angle_data(offsets, steps, 2 * i + (j >> 2))
    lane = lax.broadcasted_iota(jnp.int32, (1, 128), 1)

    def pack(r, c):
        ws = window_start(offset, u, v, low, r, c)
        shift = ws & 127
        back = (128 - shift) & 127
        blocks = filt[pl.ds(ws >> 7, 4)]
        rolled = [pltpu.roll(blocks[n], back, 1) for n in range(4)]
        return [jnp.where(lane < 128 - shift, rolled[n], rolled[n + 1]) for n in range(3)]

    def partner(p, dx, dy):
        xt, yt, zt = (x + dx) & 3, (y + dy) & 3, (z + dx + p) & 3
        return 4 * (zt & 1) + xt, 4 * (zt >> 1) + yt

    def window_copy(p, dx, dy):
        r, c = partner(p, dx, dy)
        return pltpu.make_async_remote_copy(
            src_ref=packed.at[p, 4 * dx + dy],
            dst_ref=own.at[p, 4 * dx + y],
            send_sem=win_send.at[p],
            recv_sem=win_recv.at[p],
            device_id=(2 * r + core, c),
            device_id_type=MESH,
        )

    def stage_copy(p, count=16):
        return pltpu.make_async_remote_copy(
            src_ref=packed.at[p, pl.ds(16 - count, count)],
            dst_ref=own.at[p, pl.ds(0, count)],
            send_sem=win_send.at[p],
            recv_sem=win_recv.at[p],
            device_id=sibling,
            device_id_type=MESH,
        )

    def pack_row(p, dy):
        for dx in range(4):
            for n, block in enumerate(pack(*partner(p, dx, dy))):
                packed[p, 4 * dx + dy, n] = block

    pack_row(0, 0)
    for dx in range(1, 4):
        window_copy(0, dx, 0).start()
    own[0, y] = packed[0, 0]

    @pl.loop(1, 16)
    def _(t):
        p, dy = t >> 2, t & 3
        pack_row(p, dy)
        for dx in range(4):
            window_copy(p, dx, dy).start()

    def source_angle(p, side, dx):
        xs, zs = (x - dx) & 3, (z - dx - p) & 3
        return 4 * (4 * (zs & 1) + xs) + 2 * (core ^ side) + (zs >> 1)

    pixel = lax.broadcasted_iota(jnp.int32, (1, TILE * TILE), 1)
    px = (pixel & (TILE - 1)).astype(jnp.float32) * 0.0625
    py = (pixel >> 5).astype(jnp.float32) * 0.0625
    slot = lax.broadcasted_iota(jnp.int32, (128, TILE * TILE), 0).astype(jnp.float32)

    @pl.loop(0, 8)
    def _(stage):
        for dx in range(4):
            offset, u, v, low = angle_data(offsets, steps, source_angle(stage >> 1, stage & 1, dx))
            first = ((offset + low * (TILE - 1)) & 15) - low * (TILE - 1)
            where = first.astype(jnp.float32) * 0.0625 + u.astype(jnp.float32) * px + v.astype(jnp.float32) * py
            weights[stage, pl.ds(128 * dx, 128)] = jnp.maximum(1.0 - jnp.abs(slot - where), 0.0).astype(jnp.bfloat16)

    def share_copy(p):
        return pltpu.make_async_remote_copy(
            src_ref=own.at[p],
            dst_ref=sib.at[p],
            send_sem=sib_send.at[p],
            recv_sem=sib_recv.at[p],
            device_id=sibling,
            device_id_type=MESH,
        )

    def prepare(p, side, lhs):
        place_lhs((own, sib)[side], p, lhs, offsets, steps, lambda dx: source_angle(p, side, dx))

    def multiply(lhs, stage):
        acc[...] += jnp.dot(lhs[...], weights[stage], preferred_element_type=jnp.float32)

    acc[...] = jnp.zeros_like(acc)
    stage_copy(0, 15).wait_recv()
    share_copy(0).start()
    prepare(0, 0, lhs_0)

    @pl.loop(1, 4)
    def _(p):
        stage_copy(p).wait_recv()
        share_copy(p).start()
        prepare(p, 0, lhs_1)
        multiply(lhs_0, jnp.maximum(2 * p - 3, 0))
        share_copy(p - 1).wait_recv()
        prepare(p - 1, 1, lhs_0)
        multiply(lhs_1, 2 * p)

    share_copy(3).wait_recv()
    prepare(3, 1, lhs_1)
    multiply(lhs_0, 5)

    @pl.loop(0, 4)
    def _(part):
        at = pl.ds(pl.multiple_of(256 * part, 256), 256)
        total = acc[:, at] + jnp.dot(lhs_1[...], weights[7, :, at], preferred_element_type=jnp.float32)
        store_rows(total, out, 8 * part)

    for c in row_copies:
        c.wait_send()
    for p in range(4):
        share_copy(p).wait_send()
        stage_copy(p, 15 if p == 0 else 16).wait_send()


def shards(sinogram, offsets, steps):
    vmem = pl.BlockSpec(memory_space=pltpu.VMEM)
    hbm = pl.BlockSpec(memory_space=pltpu.HBM)
    window = (3, GROUP, 128)
    return pl.pallas_call(
        whole_kernel,
        out_shape=jax.ShapeDtypeStruct((ROWS, SLICES, COLS), jnp.bfloat16),
        in_specs=[hbm, hbm, hbm],
        out_specs=vmem,
        scratch_shapes=[
            pltpu.SMEM((ANGLES,), jnp.int32),
            pltpu.SMEM((2, ANGLES), jnp.int32),
            pltpu.VMEM((IMGD, GROUP, BINS // IMGD), jnp.bfloat16),
            pltpu.VMEM((4, 16, *window), jnp.bfloat16),
            *([pltpu.VMEM((4, 16, *window), jnp.bfloat16)] * 2),
            pltpu.VMEM((64, 128, 128), jnp.bfloat16),
            pltpu.VMEM((2, 7, 128, 128), jnp.bfloat16),
            pltpu.VMEM((16, GROUP, 256), jnp.float32),
            pltpu.VMEM((36, GROUP, 128), jnp.bfloat16),
            pltpu.VMEM((8, 512, TILE * TILE), jnp.bfloat16),
            pltpu.VMEM((TILES * SLICES, 512), jnp.bfloat16),
            pltpu.VMEM((TILES * SLICES, 512), jnp.bfloat16),
            pltpu.VMEM((TILES * SLICES, TILE * TILE), jnp.float32),
            pltpu.SemaphoreType.DMA((3,)),
            pltpu.SemaphoreType.DMA((IMGD,)),
            pltpu.SemaphoreType.DMA((IMGD,)),
            pltpu.SemaphoreType.DMA((4,)),
            pltpu.SemaphoreType.DMA((4,)),
            pltpu.SemaphoreType.DMA((4,)),
            pltpu.SemaphoreType.DMA((4,)),
        ],
        compiler_params=pltpu.CompilerParams(collective_id=0, has_side_effects=True, vmem_limit_bytes=LIMIT),
        name="back_projection",
    )(
        pltpu.with_memory_space_constraint(offsets, pltpu.HBM),
        pltpu.with_memory_space_constraint(steps.T, pltpu.HBM),
        pltpu.with_memory_space_constraint(sinogram.reshape(IMGD, GROUP, BINS // IMGD), pltpu.HBM),
    )


def solution(mesh):
    return jax.shard_map(
        shards,
        mesh=mesh,
        in_specs=(P("ang", None, "img"), P(), P()),
        out_specs=P("ang", None, "img"),
        check_vma=False,
    )
```

```python
import math

import jax
import jax.numpy as jnp
from jax import lax
from jax.experimental import pallas as pl
from jax.experimental.pallas import tpu as pltpu
from jax.sharding import PartitionSpec as P

BINS = 4096
IMG = 1024
ANGLES = 32
SLICES = 64
ANG = 16
IMGD = 8
ROWS = IMG // ANG
COLS = IMG // IMGD
TILE = 32
TILES = 8
GROUP = 16
MESH = pl.DeviceIdType.MESH
LIMIT = 48 * 1024 * 1024


def ramp_tiles(ramp_hi, ramp_fine):
    gap = lax.broadcasted_iota(jnp.int32, (128, 128), 1) - lax.broadcasted_iota(jnp.int32, (128, 128), 0)
    scale = jnp.where((gap & 1) != 0, jnp.float32(-1.0 / math.pi**2), jnp.float32(0.0))
    gap_f = gap.astype(jnp.float32)

    def value(e):
        t = gap_f + jnp.asarray(128 * e).astype(jnp.float32)
        t = jnp.where(t == 0.0, jnp.float32(1.0), t)
        return scale / (t * t)

    @pl.loop(0, 64)
    def _(e):
        ramp_hi[e] = value(e - 32).astype(jnp.bfloat16)

    for e in range(-3, 4):
        v = value(e)
        if e == 0:
            v = jnp.where(gap == 0, jnp.float32(0.25), v)
        hi = v.astype(jnp.bfloat16)
        rest = v - hi.astype(jnp.float32)
        mid = rest.astype(jnp.bfloat16)
        low = (rest - mid.astype(jnp.float32)).astype(jnp.bfloat16)
        ramp_hi[e + 32] = hi
        ramp_fine[0, e + 3] = mid
        ramp_fine[1, e + 3] = low


def toeplitz(tiles, at):
    top = jnp.concatenate([tiles[at], tiles[at + 1]], axis=1)
    low = jnp.concatenate([tiles[at - 1], tiles[at]], axis=1)
    return jnp.concatenate([top, low], axis=0)


def filter_rows(rows, acc, filt, ramp_hi, ramp_fine):
    for d in sorted(range(-15, 16), key=abs):
        count = 16 - abs(d)
        first = max(0, -d)
        lhs = jnp.concatenate(
            [rows[b // 2, :, pl.ds(256 * (b % 2), 256)] for b in range(first, first + count)], axis=0
        )
        total = jnp.dot(lhs, toeplitz(ramp_hi, 2 * d + 32), preferred_element_type=jnp.float32)
        if abs(d) <= 1:
            for term in range(2):
                total += jnp.dot(
                    lhs, toeplitz(ramp_fine.at[term], 2 * d + 3), preferred_element_type=jnp.float32
                )
        total = total.reshape(count, GROUP, 256)
        if d == 0:
            acc[...] = total
        else:
            acc[pl.ds(max(0, d), count)] += total
    for b in range(16):
        for h in range(2):
            filt[2 * b + h] = acc[b, :, pl.ds(128 * h, 128)].astype(jnp.bfloat16)
    filt[pl.ds(32, 4)] = jnp.zeros((4, GROUP, 128), jnp.bfloat16)


def angle_data(offsets, steps, a):
    u = steps[0, a]
    v = steps[1, a]
    return offsets[a], u, v, jnp.minimum(u, 0) + jnp.minimum(v, 0)


def window_start(offset, u, v, low, chip_row, img):
    return (offset + u * (COLS * img) + v * (2 * ROWS * chip_row) + low * 127) >> 4


def place_lhs(windows, p, lhs, offsets, steps, angle_of):
    i = lax.axis_index("ang")
    j = lax.axis_index("img")
    lane = lax.broadcasted_iota(jnp.int32, (1, 128), 1)
    for dx in range(4):
        offset, u, v, low = angle_data(offsets, steps, angle_of(dx))
        ws = window_start(offset, u, v, low, i >> 1, j)
        base = offset + u * (COLS * j) + v * (ROWS * i) + low * (TILE - 1)
        blocks = [windows[p, pl.ds(4 * dx, 4), n].reshape(SLICES, 128) for n in range(3)]
        for tile in range(TILES):
            ty, tx = tile // 4, tile % 4
            begin = ((base + u * (TILE * tx) + v * (TILE * ty)) >> 4) - ws
            back = (128 - (begin & 127)) & 127
            left = jnp.where(begin < 128, blocks[0], jnp.where(begin < 256, blocks[1], blocks[2]))
            right = jnp.where(begin < 128, blocks[1], blocks[2])
            left = pltpu.roll(left, back, 1)
            right = pltpu.roll(right, back, 1)
            band = jnp.where(lane < 128 - (begin & 127), left, right)
            lhs[pl.ds(tile * SLICES, SLICES), pl.ds(128 * dx, 128)] = band


def store_rows(values, out, first):
    lane = lax.broadcasted_iota(jnp.int32, (1, 128), 1)
    scale = jnp.float32(2.0 / math.sqrt(ANGLES))
    near = lane < 64
    even = (lane & 32) == 0
    values = (values * scale).astype(jnp.bfloat16)
    for g in range(values.shape[1] // 128):
        for ty in range(2):
            v = [
                values[(ty * 4 + tx) * SLICES : (ty * 4 + tx + 1) * SLICES, g * 128 : g * 128 + 128]
                for tx in range(4)
            ]
            for t in range(2):
                p, q = v[t], v[t + 2]
                v[t] = jnp.where(near, p, pltpu.roll(q, 64, 1))
                v[t + 2] = jnp.where(near, pltpu.roll(p, 64, 1), q)
            for t in (0, 2):
                p, q = v[t], v[t + 1]
                v[t] = jnp.where(even, p, pltpu.roll(q, 32, 1))
                v[t + 1] = jnp.where(even, pltpu.roll(p, 96, 1), q)
            for q in range(4):
                out[TILE * ty + first + 4 * g + q] = v[q]


def whole_kernel(
    offsets_in,
    steps_in,
    sino,
    out,
    offsets,
    steps,
    rows,
    packed,
    own,
    sib,
    ramp_hi,
    ramp_fine,
    filt_acc,
    filt,
    weights,
    lhs_0,
    lhs_1,
    acc,
    local_sem,
    row_send,
    row_recv,
    win_send,
    win_recv,
    sib_send,
    sib_recv,
):
    i = lax.axis_index("ang")
    j = lax.axis_index("img")
    core = i & 1
    row = i >> 1
    x, y, z = row & 3, j & 3, 2 * (j >> 2) + (row >> 2)
    sibling = (i + 1 - 2 * core, j)

    barrier = pltpu.get_barrier_semaphore()
    for k in range(1, IMGD):
        pl.semaphore_signal(barrier, inc=1, device_id=(i, (j + k) & 7), device_id_type=MESH)
    for k in range(1, IMGD):
        pl.semaphore_signal(barrier, inc=1, device_id=((i + 2 * k) & 15, j), device_id_type=MESH)
    pl.semaphore_signal(barrier, inc=1, device_id=sibling, device_id_type=MESH)
    local = [
        pltpu.make_async_copy(offsets_in, offsets, local_sem.at[0]),
        pltpu.make_async_copy(steps_in, steps, local_sem.at[1]),
        pltpu.make_async_copy(sino.at[j], rows.at[j], local_sem.at[2]),
    ]
    for c in local:
        c.start()
    pl.semaphore_wait(barrier, 15)

    def row_copy(k):
        to = (j + k) & 7
        return pltpu.make_async_remote_copy(
            src_ref=sino.at[to],
            dst_ref=rows.at[j],
            send_sem=row_send.at[k],
            recv_sem=row_recv.at[k],
            device_id=(i, to),
            device_id_type=MESH,
        )

    row_copies = [row_copy(k) for k in range(1, IMGD)]
    for c in row_copies:
        c.start()
    for c in local:
        c.wait()
    ramp_tiles(ramp_hi, ramp_fine)

    for c in row_copies:
        c.wait_recv()
    filter_rows(rows, filt_acc, filt, ramp_hi, ramp_fine)

    offset, u, v, low = angle_data(offsets, steps, 2 * i + (j >> 2))
    lane = lax.broadcasted_iota(jnp.int32, (1, 128), 1)

    def pack(r, c):
        ws = window_start(offset, u, v, low, r, c)
        shift = ws & 127
        back = (128 - shift) & 127
        blocks = filt[pl.ds(ws >> 7, 4)]
        rolled = [pltpu.roll(blocks[n], back, 1) for n in range(4)]
        return [jnp.where(lane < 128 - shift, rolled[n], rolled[n + 1]) for n in range(3)]

    def partner(p, dx, dy):
        xt, yt, zt = (x + dx) & 3, (y + dy) & 3, (z + dx + p) & 3
        return 4 * (zt & 1) + xt, 4 * (zt >> 1) + yt

    def window_copy(p, dx, dy):
        r, c = partner(p, dx, dy)
        return pltpu.make_async_remote_copy(
            src_ref=packed.at[p, 4 * dx + dy],
            dst_ref=own.at[p, 4 * dx + y],
            send_sem=win_send.at[p],
            recv_sem=win_recv.at[p],
            device_id=(2 * r + core, c),
            device_id_type=MESH,
        )

    def stage_copy(p, count=16):
        return pltpu.make_async_remote_copy(
            src_ref=packed.at[p, pl.ds(16 - count, count)],
            dst_ref=own.at[p, pl.ds(0, count)],
            send_sem=win_send.at[p],
            recv_sem=win_recv.at[p],
            device_id=sibling,
            device_id_type=MESH,
        )

    def pack_row(p, dy):
        for dx in range(4):
            for n, block in enumerate(pack(*partner(p, dx, dy))):
                packed[p, 4 * dx + dy, n] = block

    pack_row(0, 0)
    for dx in range(1, 4):
        window_copy(0, dx, 0).start()
    own[0, y] = packed[0, 0]

    @pl.loop(1, 16)
    def _(t):
        p, dy = t >> 2, t & 3
        pack_row(p, dy)
        for dx in range(4):
            window_copy(p, dx, dy).start()

    def source_angle(p, side, dx):
        xs, zs = (x - dx) & 3, (z - dx - p) & 3
        return 4 * (4 * (zs & 1) + xs) + 2 * (core ^ side) + (zs >> 1)

    pixel = lax.broadcasted_iota(jnp.int32, (1, TILE * TILE), 1)
    px = (pixel & (TILE - 1)).astype(jnp.float32) * 0.0625
    py = (pixel >> 5).astype(jnp.float32) * 0.0625
    slot = lax.broadcasted_iota(jnp.int32, (128, TILE * TILE), 0).astype(jnp.float32)

    @pl.loop(0, 8)
    def _(stage):
        for dx in range(4):
            offset, u, v, low = angle_data(offsets, steps, source_angle(stage >> 1, stage & 1, dx))
            first = ((offset + low * (TILE - 1)) & 15) - low * (TILE - 1)
            where = first.astype(jnp.float32) * 0.0625 + u.astype(jnp.float32) * px + v.astype(jnp.float32) * py
            weights[stage, pl.ds(128 * dx, 128)] = jnp.maximum(1.0 - jnp.abs(slot - where), 0.0).astype(jnp.bfloat16)

    def share_copy(p):
        return pltpu.make_async_remote_copy(
            src_ref=own.at[p],
            dst_ref=sib.at[p],
            send_sem=sib_send.at[p],
            recv_sem=sib_recv.at[p],
            device_id=sibling,
            device_id_type=MESH,
        )

    def prepare(p, side, lhs):
        place_lhs((own, sib)[side], p, lhs, offsets, steps, lambda dx: source_angle(p, side, dx))

    def multiply(lhs, stage):
        acc[...] += jnp.dot(lhs[...], weights[stage], preferred_element_type=jnp.float32)

    acc[...] = jnp.zeros_like(acc)
    stage_copy(0, 15).wait_recv()
    share_copy(0).start()
    prepare(0, 0, lhs_0)

    @pl.loop(1, 4)
    def _(p):
        stage_copy(p).wait_recv()
        share_copy(p).start()
        prepare(p, 0, lhs_1)
        multiply(lhs_0, jnp.maximum(2 * p - 3, 0))
        share_copy(p - 1).wait_recv()
        prepare(p - 1, 1, lhs_0)
        multiply(lhs_1, 2 * p)

    multiply(lhs_0, 5)
    share_copy(3).wait_recv()
    prepare(3, 1, lhs_1)

    @pl.loop(0, 4)
    def _(part):
        at = pl.ds(pl.multiple_of(256 * part, 256), 256)
        total = acc[:, at] + jnp.dot(lhs_1[...], weights[7, :, at], preferred_element_type=jnp.float32)
        store_rows(total, out, 8 * part)

    for c in row_copies:
        c.wait_send()
    for p in range(4):
        share_copy(p).wait_send()
        stage_copy(p, 15 if p == 0 else 16).wait_send()


def shards(sinogram, offsets, steps):
    vmem = pl.BlockSpec(memory_space=pltpu.VMEM)
    hbm = pl.BlockSpec(memory_space=pltpu.HBM)
    window = (3, GROUP, 128)
    return pl.pallas_call(
        whole_kernel,
        out_shape=jax.ShapeDtypeStruct((ROWS, SLICES, COLS), jnp.bfloat16),
        in_specs=[hbm, hbm, hbm],
        out_specs=vmem,
        scratch_shapes=[
            pltpu.SMEM((ANGLES,), jnp.int32),
            pltpu.SMEM((2, ANGLES), jnp.int32),
            pltpu.VMEM((IMGD, GROUP, BINS // IMGD), jnp.bfloat16),
            pltpu.VMEM((4, 16, *window), jnp.bfloat16),
            *([pltpu.VMEM((4, 16, *window), jnp.bfloat16)] * 2),
            pltpu.VMEM((64, 128, 128), jnp.bfloat16),
            pltpu.VMEM((2, 7, 128, 128), jnp.bfloat16),
            pltpu.VMEM((16, GROUP, 256), jnp.float32),
            pltpu.VMEM((36, GROUP, 128), jnp.bfloat16),
            pltpu.VMEM((8, 512, TILE * TILE), jnp.bfloat16),
            pltpu.VMEM((TILES * SLICES, 512), jnp.bfloat16),
            pltpu.VMEM((TILES * SLICES, 512), jnp.bfloat16),
            pltpu.VMEM((TILES * SLICES, TILE * TILE), jnp.float32),
            pltpu.SemaphoreType.DMA((3,)),
            pltpu.SemaphoreType.DMA((IMGD,)),
            pltpu.SemaphoreType.DMA((IMGD,)),
            pltpu.SemaphoreType.DMA((4,)),
            pltpu.SemaphoreType.DMA((4,)),
            pltpu.SemaphoreType.DMA((4,)),
            pltpu.SemaphoreType.DMA((4,)),
        ],
        compiler_params=pltpu.CompilerParams(collective_id=0, has_side_effects=True, vmem_limit_bytes=LIMIT),
        name="back_projection",
    )(
        pltpu.with_memory_space_constraint(offsets, pltpu.HBM),
        pltpu.with_memory_space_constraint(steps.T, pltpu.HBM),
        pltpu.with_memory_space_constraint(sinogram.reshape(IMGD, GROUP, BINS // IMGD), pltpu.HBM),
    )


def solution(mesh):
    return jax.shard_map(
        shards,
        mesh=mesh,
        in_specs=(P("ang", None, "img"), P(), P()),
        out_specs=P("ang", None, "img"),
        check_vma=False,
    )
```

```python
import math

import jax
import jax.numpy as jnp
from jax import lax
from jax.experimental import pallas as pl
from jax.experimental.pallas import tpu as pltpu
from jax.sharding import PartitionSpec as P

BINS = 4096
IMG = 1024
ANGLES = 32
SLICES = 64
ANG = 16
IMGD = 8
ROWS = IMG // ANG
COLS = IMG // IMGD
TILE = 32
TILES = 8
GROUP = 16
MESH = pl.DeviceIdType.MESH
LIMIT = 48 * 1024 * 1024


def ramp_tiles(ramp_hi, ramp_fine):
    gap = lax.broadcasted_iota(jnp.int32, (128, 128), 1) - lax.broadcasted_iota(jnp.int32, (128, 128), 0)
    scale = jnp.where((gap & 1) != 0, jnp.float32(-1.0 / math.pi**2), jnp.float32(0.0))
    gap_f = gap.astype(jnp.float32)

    def value(e):
        t = gap_f + jnp.asarray(128 * e).astype(jnp.float32)
        t = jnp.where(t == 0.0, jnp.float32(1.0), t)
        return scale / (t * t)

    @pl.loop(0, 64)
    def _(e):
        ramp_hi[e] = value(e - 32).astype(jnp.bfloat16)

    for e in range(-3, 4):
        v = value(e)
        if e == 0:
            v = jnp.where(gap == 0, jnp.float32(0.25), v)
        hi = v.astype(jnp.bfloat16)
        rest = v - hi.astype(jnp.float32)
        mid = rest.astype(jnp.bfloat16)
        low = (rest - mid.astype(jnp.float32)).astype(jnp.bfloat16)
        ramp_hi[e + 32] = hi
        ramp_fine[0, e + 3] = mid
        ramp_fine[1, e + 3] = low


def toeplitz(tiles, at):
    top = jnp.concatenate([tiles[at], tiles[at + 1]], axis=1)
    low = jnp.concatenate([tiles[at - 1], tiles[at]], axis=1)
    return jnp.concatenate([top, low], axis=0)


def filter_rows(rows, acc, filt, ramp_hi, ramp_fine):
    for d in sorted(range(-15, 16), key=abs):
        count = 16 - abs(d)
        first = max(0, -d)
        lhs = jnp.concatenate(
            [rows[b // 2, :, pl.ds(256 * (b % 2), 256)] for b in range(first, first + count)], axis=0
        )
        total = jnp.dot(lhs, toeplitz(ramp_hi, 2 * d + 32), preferred_element_type=jnp.float32)
        if abs(d) <= 1:
            for term in range(2):
                total += jnp.dot(
                    lhs, toeplitz(ramp_fine.at[term], 2 * d + 3), preferred_element_type=jnp.float32
                )
        total = total.reshape(count, GROUP, 256)
        if d == 0:
            acc[...] = total
        else:
            acc[pl.ds(max(0, d), count)] += total
    for b in range(16):
        for h in range(2):
            filt[2 * b + h] = acc[b, :, pl.ds(128 * h, 128)].astype(jnp.bfloat16)
    filt[pl.ds(32, 4)] = jnp.zeros((4, GROUP, 128), jnp.bfloat16)


def angle_data(offsets, steps, a):
    u = steps[0, a]
    v = steps[1, a]
    return offsets[a], u, v, jnp.minimum(u, 0) + jnp.minimum(v, 0)


def window_start(offset, u, v, low, chip_row, img):
    return (offset + u * (COLS * img) + v * (2 * ROWS * chip_row) + low * 127) >> 4


def place_lhs(windows, p, lhs, offsets, steps, angle_of):
    i = lax.axis_index("ang")
    j = lax.axis_index("img")
    lane = lax.broadcasted_iota(jnp.int32, (1, 128), 1)
    for dx in range(4):
        offset, u, v, low = angle_data(offsets, steps, angle_of(dx))
        ws = window_start(offset, u, v, low, i >> 1, j)
        base = offset + u * (COLS * j) + v * (ROWS * i) + low * (TILE - 1)
        blocks = [windows[p, pl.ds(4 * dx, 4), n].reshape(SLICES, 128) for n in range(3)]
        for tile in range(TILES):
            ty, tx = tile // 4, tile % 4
            begin = ((base + u * (TILE * tx) + v * (TILE * ty)) >> 4) - ws
            back = (128 - (begin & 127)) & 127
            left = jnp.where(begin < 128, blocks[0], jnp.where(begin < 256, blocks[1], blocks[2]))
            right = jnp.where(begin < 128, blocks[1], blocks[2])
            left = pltpu.roll(left, back, 1)
            right = pltpu.roll(right, back, 1)
            band = jnp.where(lane < 128 - (begin & 127), left, right)
            lhs[pl.ds(tile * SLICES, SLICES), pl.ds(128 * dx, 128)] = band


def store_rows(values, out, first):
    lane = lax.broadcasted_iota(jnp.int32, (1, 128), 1)
    scale = jnp.float32(2.0 / math.sqrt(ANGLES))
    near = lane < 64
    even = (lane & 32) == 0
    values = (values * scale).astype(jnp.bfloat16)
    for g in range(values.shape[1] // 128):
        for ty in range(2):
            v = [
                values[(ty * 4 + tx) * SLICES : (ty * 4 + tx + 1) * SLICES, g * 128 : g * 128 + 128]
                for tx in range(4)
            ]
            for t in range(2):
                p, q = v[t], v[t + 2]
                v[t] = jnp.where(near, p, pltpu.roll(q, 64, 1))
                v[t + 2] = jnp.where(near, pltpu.roll(p, 64, 1), q)
            for t in (0, 2):
                p, q = v[t], v[t + 1]
                v[t] = jnp.where(even, p, pltpu.roll(q, 32, 1))
                v[t + 1] = jnp.where(even, pltpu.roll(p, 96, 1), q)
            for q in range(4):
                out[TILE * ty + first + 4 * g + q] = v[q]


def whole_kernel(
    offsets_in,
    steps_in,
    sino,
    out,
    offsets,
    steps,
    rows,
    packed,
    own,
    sib,
    ramp_hi,
    ramp_fine,
    filt_acc,
    filt,
    weights,
    lhs_0,
    lhs_1,
    acc,
    local_sem,
    row_send,
    row_recv,
    win_send,
    win_recv,
    sib_send,
    sib_recv,
):
    i = lax.axis_index("ang")
    j = lax.axis_index("img")
    core = i & 1
    row = i >> 1
    x, y, z = row & 3, j & 3, 2 * (j >> 2) + (row >> 2)
    sibling = (i + 1 - 2 * core, j)

    barrier = pltpu.get_barrier_semaphore()
    for k in range(1, IMGD):
        pl.semaphore_signal(barrier, inc=1, device_id=(i, (j + k) & 7), device_id_type=MESH)
    for k in range(1, IMGD):
        pl.semaphore_signal(barrier, inc=1, device_id=((i + 2 * k) & 15, j), device_id_type=MESH)
    pl.semaphore_signal(barrier, inc=1, device_id=sibling, device_id_type=MESH)
    local = [
        pltpu.make_async_copy(offsets_in, offsets, local_sem.at[0]),
        pltpu.make_async_copy(steps_in, steps, local_sem.at[1]),
        pltpu.make_async_copy(sino.at[j], rows.at[j], local_sem.at[2]),
    ]
    for c in local:
        c.start()
    pl.semaphore_wait(barrier, 15)

    def row_copy(k):
        to = (j + k) & 7
        return pltpu.make_async_remote_copy(
            src_ref=sino.at[to],
            dst_ref=rows.at[j],
            send_sem=row_send.at[k],
            recv_sem=row_recv.at[k],
            device_id=(i, to),
            device_id_type=MESH,
        )

    row_copies = [row_copy(k) for k in range(1, IMGD)]
    for c in row_copies:
        c.start()
    for c in local:
        c.wait()
    ramp_tiles(ramp_hi, ramp_fine)

    for c in row_copies:
        c.wait_recv()
    filter_rows(rows, filt_acc, filt, ramp_hi, ramp_fine)

    offset, u, v, low = angle_data(offsets, steps, 2 * i + (j >> 2))
    lane = lax.broadcasted_iota(jnp.int32, (1, 128), 1)

    def pack(r, c):
        ws = window_start(offset, u, v, low, r, c)
        shift = ws & 127
        back = (128 - shift) & 127
        blocks = filt[pl.ds(ws >> 7, 4)]
        rolled = [pltpu.roll(blocks[n], back, 1) for n in range(4)]
        return [jnp.where(lane < 128 - shift, rolled[n], rolled[n + 1]) for n in range(3)]

    def partner(p, dx, dy):
        xt, yt, zt = (x + dx) & 3, (y + dy) & 3, (z + dx + p) & 3
        return 4 * (zt & 1) + xt, 4 * (zt >> 1) + yt

    def window_copy(p, dx, dy):
        r, c = partner(p, dx, dy)
        return pltpu.make_async_remote_copy(
            src_ref=packed.at[p, 4 * dx + dy],
            dst_ref=own.at[p, 4 * dx + y],
            send_sem=win_send.at[p],
            recv_sem=win_recv.at[p],
            device_id=(2 * r + core, c),
            device_id_type=MESH,
        )

    def stage_copy(p, count=16):
        return pltpu.make_async_remote_copy(
            src_ref=packed.at[p, pl.ds(16 - count, count)],
            dst_ref=own.at[p, pl.ds(0, count)],
            send_sem=win_send.at[p],
            recv_sem=win_recv.at[p],
            device_id=sibling,
            device_id_type=MESH,
        )

    def pack_row(p, dy):
        for dx in range(4):
            for n, block in enumerate(pack(*partner(p, dx, dy))):
                packed[p, 4 * dx + dy, n] = block

    pack_row(0, 0)
    for dx in range(1, 4):
        window_copy(0, dx, 0).start()
    own[0, y] = packed[0, 0]

    @pl.loop(1, 16)
    def _(t):
        p, dy = t >> 2, t & 3
        pack_row(p, dy)
        for dx in range(4):
            window_copy(p, dx, dy).start()

    def source_angle(p, side, dx):
        xs, zs = (x - dx) & 3, (z - dx - p) & 3
        return 4 * (4 * (zs & 1) + xs) + 2 * (core ^ side) + (zs >> 1)

    pixel = lax.broadcasted_iota(jnp.int32, (1, TILE * TILE), 1)
    px = (pixel & (TILE - 1)).astype(jnp.float32) * 0.0625
    py = (pixel >> 5).astype(jnp.float32) * 0.0625
    slot = lax.broadcasted_iota(jnp.int32, (128, TILE * TILE), 0).astype(jnp.float32)

    @pl.loop(0, 8)
    def _(stage):
        for dx in range(4):
            offset, u, v, low = angle_data(offsets, steps, source_angle(stage >> 1, stage & 1, dx))
            first = ((offset + low * (TILE - 1)) & 15) - low * (TILE - 1)
            where = first.astype(jnp.float32) * 0.0625 + u.astype(jnp.float32) * px + v.astype(jnp.float32) * py
            weights[stage, pl.ds(128 * dx, 128)] = jnp.maximum(1.0 - jnp.abs(slot - where), 0.0).astype(jnp.bfloat16)

    def share_copy(p):
        return pltpu.make_async_remote_copy(
            src_ref=own.at[p],
            dst_ref=sib.at[p],
            send_sem=sib_send.at[p],
            recv_sem=sib_recv.at[p],
            device_id=sibling,
            device_id_type=MESH,
        )

    def prepare(p, side, lhs):
        place_lhs((own, sib)[side], p, lhs, offsets, steps, lambda dx: source_angle(p, side, dx))

    def multiply(lhs, stage):
        acc[...] += jnp.dot(lhs[...], weights[stage], preferred_element_type=jnp.float32)

    acc[...] = jnp.zeros_like(acc)
    stage_copy(0, 15).wait_recv()
    share_copy(0).start()
    prepare(0, 0, lhs_0)

    @pl.loop(1, 4)
    def _(p):
        stage_copy(p).wait_recv()
        share_copy(p).start()
        prepare(p, 0, lhs_1)
        multiply(lhs_0, jnp.maximum(2 * p - 3, 0))
        share_copy(p - 1).wait_recv()
        prepare(p - 1, 1, lhs_0)
        multiply(lhs_1, 2 * p)

    multiply(lhs_0, 5)
    share_copy(3).wait_recv()
    prepare(3, 1, lhs_1)

    @pl.loop(0, 2)
    def _(part):
        at = pl.ds(pl.multiple_of(512 * part, 512), 512)
        total = acc[:, at] + jnp.dot(lhs_1[...], weights[7, :, at], preferred_element_type=jnp.float32)
        store_rows(total, out, 16 * part)

    for c in row_copies:
        c.wait_send()
    for p in range(4):
        share_copy(p).wait_send()
        stage_copy(p, 15 if p == 0 else 16).wait_send()


def shards(sinogram, offsets, steps):
    vmem = pl.BlockSpec(memory_space=pltpu.VMEM)
    hbm = pl.BlockSpec(memory_space=pltpu.HBM)
    window = (3, GROUP, 128)
    return pl.pallas_call(
        whole_kernel,
        out_shape=jax.ShapeDtypeStruct((ROWS, SLICES, COLS), jnp.bfloat16),
        in_specs=[hbm, hbm, hbm],
        out_specs=vmem,
        scratch_shapes=[
            pltpu.SMEM((ANGLES,), jnp.int32),
            pltpu.SMEM((2, ANGLES), jnp.int32),
            pltpu.VMEM((IMGD, GROUP, BINS // IMGD), jnp.bfloat16),
            pltpu.VMEM((4, 16, *window), jnp.bfloat16),
            *([pltpu.VMEM((4, 16, *window), jnp.bfloat16)] * 2),
            pltpu.VMEM((64, 128, 128), jnp.bfloat16),
            pltpu.VMEM((2, 7, 128, 128), jnp.bfloat16),
            pltpu.VMEM((16, GROUP, 256), jnp.float32),
            pltpu.VMEM((36, GROUP, 128), jnp.bfloat16),
            pltpu.VMEM((8, 512, TILE * TILE), jnp.bfloat16),
            pltpu.VMEM((TILES * SLICES, 512), jnp.bfloat16),
            pltpu.VMEM((TILES * SLICES, 512), jnp.bfloat16),
            pltpu.VMEM((TILES * SLICES, TILE * TILE), jnp.float32),
            pltpu.SemaphoreType.DMA((3,)),
            pltpu.SemaphoreType.DMA((IMGD,)),
            pltpu.SemaphoreType.DMA((IMGD,)),
            pltpu.SemaphoreType.DMA((4,)),
            pltpu.SemaphoreType.DMA((4,)),
            pltpu.SemaphoreType.DMA((4,)),
            pltpu.SemaphoreType.DMA((4,)),
        ],
        compiler_params=pltpu.CompilerParams(collective_id=0, has_side_effects=True, vmem_limit_bytes=LIMIT),
        name="back_projection",
    )(
        pltpu.with_memory_space_constraint(offsets, pltpu.HBM),
        pltpu.with_memory_space_constraint(steps.T, pltpu.HBM),
        pltpu.with_memory_space_constraint(sinogram.reshape(IMGD, GROUP, BINS // IMGD), pltpu.HBM),
    )


def solution(mesh):
    return jax.shard_map(
        shards,
        mesh=mesh,
        in_specs=(P("ang", None, "img"), P(), P()),
        out_specs=P("ang", None, "img"),
        check_vma=False,
    )
```

```python
import math

import jax
import jax.numpy as jnp
from jax import lax
from jax.experimental import pallas as pl
from jax.experimental.pallas import tpu as pltpu
from jax.sharding import PartitionSpec as P

BINS = 4096
IMG = 1024
ANGLES = 32
SLICES = 64
ANG = 16
IMGD = 8
ROWS = IMG // ANG
COLS = IMG // IMGD
TILE = 32
TILES = 8
GROUP = 16
MESH = pl.DeviceIdType.MESH
LIMIT = 48 * 1024 * 1024


def ramp_tiles(ramp_hi, ramp_fine):
    gap = lax.broadcasted_iota(jnp.int32, (128, 128), 1) - lax.broadcasted_iota(jnp.int32, (128, 128), 0)
    scale = jnp.where((gap & 1) != 0, jnp.float32(-1.0 / math.pi**2), jnp.float32(0.0))
    gap_f = gap.astype(jnp.float32)

    def value(e):
        t = gap_f + jnp.asarray(128 * e).astype(jnp.float32)
        t = jnp.where(t == 0.0, jnp.float32(1.0), t)
        return scale / (t * t)

    @pl.loop(0, 64)
    def _(e):
        ramp_hi[e] = value(e - 32).astype(jnp.bfloat16)

    for e in range(-3, 4):
        v = value(e)
        if e == 0:
            v = jnp.where(gap == 0, jnp.float32(0.25), v)
        hi = v.astype(jnp.bfloat16)
        rest = v - hi.astype(jnp.float32)
        mid = rest.astype(jnp.bfloat16)
        low = (rest - mid.astype(jnp.float32)).astype(jnp.bfloat16)
        ramp_hi[e + 32] = hi
        ramp_fine[0, e + 3] = mid
        ramp_fine[1, e + 3] = low


def toeplitz(tiles, at):
    top = jnp.concatenate([tiles[at], tiles[at + 1]], axis=1)
    low = jnp.concatenate([tiles[at - 1], tiles[at]], axis=1)
    return jnp.concatenate([top, low], axis=0)


def filter_rows(rows, acc, filt, ramp_hi, ramp_fine):
    for d in sorted(range(-15, 16), key=abs):
        count = 16 - abs(d)
        first = max(0, -d)
        lhs = jnp.concatenate(
            [rows[b // 2, :, pl.ds(256 * (b % 2), 256)] for b in range(first, first + count)], axis=0
        )
        total = jnp.dot(lhs, toeplitz(ramp_hi, 2 * d + 32), preferred_element_type=jnp.float32)
        if abs(d) <= 1:
            for term in range(2):
                total += jnp.dot(
                    lhs, toeplitz(ramp_fine.at[term], 2 * d + 3), preferred_element_type=jnp.float32
                )
        total = total.reshape(count, GROUP, 256)
        if d == 0:
            acc[...] = total
        else:
            acc[pl.ds(max(0, d), count)] += total
    for b in range(16):
        for h in range(2):
            filt[2 * b + h] = acc[b, :, pl.ds(128 * h, 128)].astype(jnp.bfloat16)
    filt[pl.ds(32, 4)] = jnp.zeros((4, GROUP, 128), jnp.bfloat16)


def angle_data(offsets, steps, a):
    u = steps[0, a]
    v = steps[1, a]
    return offsets[a], u, v, jnp.minimum(u, 0) + jnp.minimum(v, 0)


def window_start(offset, u, v, low, chip_row, img):
    return (offset + u * (COLS * img) + v * (2 * ROWS * chip_row) + low * 127) >> 4


def place_lhs(windows, p, lhs, offsets, steps, angle_of):
    i = lax.axis_index("ang")
    j = lax.axis_index("img")
    lane = lax.broadcasted_iota(jnp.int32, (1, 128), 1)
    for dx in range(4):
        offset, u, v, low = angle_data(offsets, steps, angle_of(dx))
        ws = window_start(offset, u, v, low, i >> 1, j)
        base = offset + u * (COLS * j) + v * (ROWS * i) + low * (TILE - 1)
        blocks = [windows[p, pl.ds(4 * dx, 4), n].reshape(SLICES, 128) for n in range(3)]
        for tile in range(TILES):
            ty, tx = tile // 4, tile % 4
            begin = ((base + u * (TILE * tx) + v * (TILE * ty)) >> 4) - ws
            back = (128 - (begin & 127)) & 127
            left = jnp.where(begin < 128, blocks[0], jnp.where(begin < 256, blocks[1], blocks[2]))
            right = jnp.where(begin < 128, blocks[1], blocks[2])
            left = pltpu.roll(left, back, 1)
            right = pltpu.roll(right, back, 1)
            band = jnp.where(lane < 128 - (begin & 127), left, right)
            lhs[pl.ds(tile * SLICES, SLICES), pl.ds(128 * dx, 128)] = band


def store_rows(values, out, first):
    lane = lax.broadcasted_iota(jnp.int32, (1, 128), 1)
    scale = jnp.float32(2.0 / math.sqrt(ANGLES))
    near = lane < 64
    even = (lane & 32) == 0
    values = (values * scale).astype(jnp.bfloat16)
    for g in range(values.shape[1] // 128):
        for ty in range(2):
            v = [
                values[(ty * 4 + tx) * SLICES : (ty * 4 + tx + 1) * SLICES, g * 128 : g * 128 + 128]
                for tx in range(4)
            ]
            for t in range(2):
                p, q = v[t], v[t + 2]
                v[t] = jnp.where(near, p, pltpu.roll(q, 64, 1))
                v[t + 2] = jnp.where(near, pltpu.roll(p, 64, 1), q)
            for t in (0, 2):
                p, q = v[t], v[t + 1]
                v[t] = jnp.where(even, p, pltpu.roll(q, 32, 1))
                v[t + 1] = jnp.where(even, pltpu.roll(p, 96, 1), q)
            for q in range(4):
                out[TILE * ty + first + 4 * g + q] = v[q]


def whole_kernel(
    offsets_in,
    steps_in,
    sino,
    out,
    offsets,
    steps,
    rows,
    packed,
    own,
    sib,
    ramp_hi,
    ramp_fine,
    filt_acc,
    filt,
    weights,
    lhs_0,
    lhs_1,
    acc,
    local_sem,
    row_send,
    row_recv,
    win_send,
    win_recv,
    sib_send,
    sib_recv,
):
    i = lax.axis_index("ang")
    j = lax.axis_index("img")
    core = i & 1
    row = i >> 1
    x, y, z = row & 3, j & 3, 2 * (j >> 2) + (row >> 2)
    sibling = (i + 1 - 2 * core, j)

    barrier = pltpu.get_barrier_semaphore()
    for k in range(1, IMGD):
        pl.semaphore_signal(barrier, inc=1, device_id=(i, (j + k) & 7), device_id_type=MESH)
    for k in range(1, IMGD):
        pl.semaphore_signal(barrier, inc=1, device_id=((i + 2 * k) & 15, j), device_id_type=MESH)
    pl.semaphore_signal(barrier, inc=1, device_id=sibling, device_id_type=MESH)
    local = [
        pltpu.make_async_copy(offsets_in, offsets, local_sem.at[0]),
        pltpu.make_async_copy(steps_in, steps, local_sem.at[1]),
        pltpu.make_async_copy(sino.at[j], rows.at[j], local_sem.at[2]),
    ]
    for c in local:
        c.start()
    pl.semaphore_wait(barrier, 15)

    def row_copy(k):
        to = (j + k) & 7
        return pltpu.make_async_remote_copy(
            src_ref=sino.at[to],
            dst_ref=rows.at[j],
            send_sem=row_send.at[k],
            recv_sem=row_recv.at[k],
            device_id=(i, to),
            device_id_type=MESH,
        )

    row_copies = [row_copy(k) for k in range(1, IMGD)]
    for c in row_copies:
        c.start()
    for c in local:
        c.wait()
    ramp_tiles(ramp_hi, ramp_fine)

    for c in row_copies:
        c.wait_recv()
    filter_rows(rows, filt_acc, filt, ramp_hi, ramp_fine)

    offset, u, v, low = angle_data(offsets, steps, 2 * i + (j >> 2))
    lane = lax.broadcasted_iota(jnp.int32, (1, 128), 1)

    def pack(r, c):
        ws = window_start(offset, u, v, low, r, c)
        shift = ws & 127
        back = (128 - shift) & 127
        blocks = filt[pl.ds(ws >> 7, 4)]
        rolled = [pltpu.roll(blocks[n], back, 1) for n in range(4)]
        return [jnp.where(lane < 128 - shift, rolled[n], rolled[n + 1]) for n in range(3)]

    def partner(p, dx, dy):
        xt, yt, zt = (x + dx) & 3, (y + dy) & 3, (z + dx + p) & 3
        return 4 * (zt & 1) + xt, 4 * (zt >> 1) + yt

    def window_copy(p, dx, dy):
        r, c = partner(p, dx, dy)
        return pltpu.make_async_remote_copy(
            src_ref=packed.at[p, 4 * dx + dy],
            dst_ref=own.at[p, 4 * dx + y],
            send_sem=win_send.at[p],
            recv_sem=win_recv.at[p],
            device_id=(2 * r + core, c),
            device_id_type=MESH,
        )

    def stage_copy(p, count=16):
        return pltpu.make_async_remote_copy(
            src_ref=packed.at[p, pl.ds(16 - count, count)],
            dst_ref=own.at[p, pl.ds(0, count)],
            send_sem=win_send.at[p],
            recv_sem=win_recv.at[p],
            device_id=sibling,
            device_id_type=MESH,
        )

    def pack_row(p, dy):
        for dx in range(4):
            for n, block in enumerate(pack(*partner(p, dx, dy))):
                packed[p, 4 * dx + dy, n] = block

    pack_row(0, 0)
    for dx in range(1, 4):
        window_copy(0, dx, 0).start()
    own[0, y] = packed[0, 0]

    @pl.loop(1, 16)
    def _(t):
        p, dy = t >> 2, t & 3
        pack_row(p, dy)
        for dx in range(4):
            window_copy(p, dx, dy).start()

    def source_angle(p, side, dx):
        xs, zs = (x - dx) & 3, (z - dx - p) & 3
        return 4 * (4 * (zs & 1) + xs) + 2 * (core ^ side) + (zs >> 1)

    pixel = lax.broadcasted_iota(jnp.int32, (1, TILE * TILE), 1)
    px = (pixel & (TILE - 1)).astype(jnp.float32) * 0.0625
    py = (pixel >> 5).astype(jnp.float32) * 0.0625
    slot = lax.broadcasted_iota(jnp.int32, (128, TILE * TILE), 0).astype(jnp.float32)

    @pl.loop(0, 8)
    def _(stage):
        for dx in range(4):
            offset, u, v, low = angle_data(offsets, steps, source_angle(stage >> 1, stage & 1, dx))
            first = ((offset + low * (TILE - 1)) & 15) - low * (TILE - 1)
            where = first.astype(jnp.float32) * 0.0625 + u.astype(jnp.float32) * px + v.astype(jnp.float32) * py
            weights[stage, pl.ds(128 * dx, 128)] = jnp.maximum(1.0 - jnp.abs(slot - where), 0.0).astype(jnp.bfloat16)

    def share_copy(p):
        return pltpu.make_async_remote_copy(
            src_ref=own.at[p],
            dst_ref=sib.at[p],
            send_sem=sib_send.at[p],
            recv_sem=sib_recv.at[p],
            device_id=sibling,
            device_id_type=MESH,
        )

    def prepare(p, side, lhs):
        place_lhs((own, sib)[side], p, lhs, offsets, steps, lambda dx: source_angle(p, side, dx))

    def multiply(lhs, stage):
        acc[...] += jnp.dot(lhs[...], weights[stage], preferred_element_type=jnp.float32)

    acc[...] = jnp.zeros_like(acc)
    stage_copy(0, 15).wait_recv()
    share_copy(0).start()
    prepare(0, 0, lhs_0)

    @pl.loop(1, 4)
    def _(p):
        stage_copy(p).wait_recv()
        share_copy(p).start()
        prepare(p, 0, lhs_1)
        multiply(lhs_0, jnp.maximum(2 * p - 3, 0))
        share_copy(p - 1).wait_recv()
        prepare(p - 1, 1, lhs_0)
        multiply(lhs_1, 2 * p)

    multiply(lhs_0, 5)
    share_copy(3).wait_recv()
    prepare(3, 1, lhs_1)

    for part in range(2):
        at = pl.ds(512 * part, 512)
        total = acc[:, at] + jnp.dot(lhs_1[...], weights[7, :, at], preferred_element_type=jnp.float32)
        store_rows(total, out, 16 * part)

    for c in row_copies:
        c.wait_send()
    for p in range(4):
        share_copy(p).wait_send()
        stage_copy(p, 15 if p == 0 else 16).wait_send()


def shards(sinogram, offsets, steps):
    vmem = pl.BlockSpec(memory_space=pltpu.VMEM)
    hbm = pl.BlockSpec(memory_space=pltpu.HBM)
    window = (3, GROUP, 128)
    return pl.pallas_call(
        whole_kernel,
        out_shape=jax.ShapeDtypeStruct((ROWS, SLICES, COLS), jnp.bfloat16),
        in_specs=[hbm, hbm, hbm],
        out_specs=vmem,
        scratch_shapes=[
            pltpu.SMEM((ANGLES,), jnp.int32),
            pltpu.SMEM((2, ANGLES), jnp.int32),
            pltpu.VMEM((IMGD, GROUP, BINS // IMGD), jnp.bfloat16),
            pltpu.VMEM((4, 16, *window), jnp.bfloat16),
            *([pltpu.VMEM((4, 16, *window), jnp.bfloat16)] * 2),
            pltpu.VMEM((64, 128, 128), jnp.bfloat16),
            pltpu.VMEM((2, 7, 128, 128), jnp.bfloat16),
            pltpu.VMEM((16, GROUP, 256), jnp.float32),
            pltpu.VMEM((36, GROUP, 128), jnp.bfloat16),
            pltpu.VMEM((8, 512, TILE * TILE), jnp.bfloat16),
            pltpu.VMEM((TILES * SLICES, 512), jnp.bfloat16),
            pltpu.VMEM((TILES * SLICES, 512), jnp.bfloat16),
            pltpu.VMEM((TILES * SLICES, TILE * TILE), jnp.float32),
            pltpu.SemaphoreType.DMA((3,)),
            pltpu.SemaphoreType.DMA((IMGD,)),
            pltpu.SemaphoreType.DMA((IMGD,)),
            pltpu.SemaphoreType.DMA((4,)),
            pltpu.SemaphoreType.DMA((4,)),
            pltpu.SemaphoreType.DMA((4,)),
            pltpu.SemaphoreType.DMA((4,)),
        ],
        compiler_params=pltpu.CompilerParams(collective_id=0, has_side_effects=True, vmem_limit_bytes=LIMIT),
        name="back_projection",
    )(
        pltpu.with_memory_space_constraint(offsets, pltpu.HBM),
        pltpu.with_memory_space_constraint(steps.T, pltpu.HBM),
        pltpu.with_memory_space_constraint(sinogram.reshape(IMGD, GROUP, BINS // IMGD), pltpu.HBM),
    )


def solution(mesh):
    return jax.shard_map(
        shards,
        mesh=mesh,
        in_specs=(P("ang", None, "img"), P(), P()),
        out_specs=P("ang", None, "img"),
        check_vma=False,
    )
```
